128 devices in a mesh: seq: 32 (over x, y, z_hi), tp: 4 (over z_lo, core).
Axes of the slice: x: 4, y: 4, z: 4 (z_hi: 2, z_lo: 2; z = z_hi * 2 + z_lo), core: 2. Of those that a mesh axis runs over, the one named last changes fastest.
Arguments:
- queries: bfloat16 [16384, 4096], P('seq', 'tp'), may hold values from -6 to 6
- token_keys: bfloat16 [16384, 4096], P('seq', 'tp'), may hold values from -6 to 6
- token_values: bfloat16 [16384, 4096], P('seq', 'tp'), may hold values from -6 to 6
- out_weight: bfloat16 [4096, 4096], P('tp'), may hold values from -0.09375 to 0.09375
- out_grad: bfloat16 [16384, 4096], P('seq'), may hold values from -6 to 6
Outputs:
- layer_out: bfloat16 [16384, 4096], P('seq', 'tp')
- query_grad: bfloat16 [16384, 4096], P('seq', 'tp')
- key_grad: bfloat16 [16384, 4096], P('seq', 'tp')
- value_grad: bfloat16 [16384, 4096], P('seq', 'tp')
- weight_grad: float32 [4096, 4096], P('tp', 'seq')
The draws below stay inside these ranges and needn't reach their ends.
All inputs are finite; a program needn't handle non-finite values.
Results may differ from the reference program's by a relative error of at most 0.024.
Values may be sent and summed in bfloat16 or wider, within the bound.
No kernel may reach another device: no remote copies, remote signals or barrier semaphores. Data moves between devices by JAX's collectives and lax.ppermute only.
A program may use at most 256 MiB of HBM per device.

```python
import math
import jax
import jax.numpy as jnp
from jax import lax

HEADS = 32
DH = 128
D = 4096
TOK_DEV = 512
FB = 128
P1 = 16
P2 = 256
HD = 4096
TOKENS = 16384
N_SEQ = 32


def base_field(field_key):
    return jax.random.truncated_normal(field_key, -6.0, 6.0, (TOKENS, HEADS * DH), jnp.float32)


def draw_queries(key, part):
    field = base_field(jax.random.fold_in(key, 101))
    return field.astype(jnp.bfloat16)


def draw_token_keys(key, part):
    field = base_field(jax.random.fold_in(key, 202))
    return field.astype(jnp.bfloat16)


def raised(entries, rng, source, target, blocks, factor):
    owner, partner = [(jnp.arange(entries.shape[dim]) // (entries.shape[dim] // blocks)).reshape([-1 if axis == dim else 1 for axis in range(entries.ndim)]) for dim in (source, target)]
    chosen = jax.random.permutation(rng, blocks)[partner]
    strong = (owner == chosen) | (owner == (partner + blocks // 2) % blocks)
    return jnp.where(strong, factor * entries, entries)


def levels(own_key, shape, cuts, low, high):
    factor_of, own = 1.0, jax.random.fold_in(own_key, 6)
    for axis_at, parts in cuts:
        draws = jnp.exp(jax.random.uniform(jax.random.fold_in(own, axis_at), (parts,), jnp.float32, low / len(cuts), high / len(cuts)))
        factor_of = factor_of * jnp.repeat(draws, shape[axis_at] // parts).reshape([-1 if axis == axis_at else 1 for axis in range(len(shape))])
    return factor_of


def noise(key, shape, width, bound, shards=(), kind=jnp.bfloat16):
    values = jax.random.normal(key, shape, jnp.float32) * width
    if len(shards) > 0:
        values = levels(key, shape, shards, -0.22, 0.18) * values
    return jnp.clip(values, min=-bound, max=bound).astype(kind)


def bell_draw_with(stream_key, shape, width, most, cuts, heavy, kind=jnp.bfloat16):
    drawn = width * jax.random.normal(stream_key, shape, jnp.float32)
    if cuts:
        drawn = drawn * levels(stream_key, shape, cuts, -0.22, 0.18)
    return jnp.clip(raised(drawn, jax.random.fold_in(stream_key, 3), *heavy), -most, most).astype(kind)


def setup_inputs(seed: int = 0) -> dict:
    streams_of = jax.random.split(jax.random.key(seed), 6)
    return {
        "queries": draw_queries(jax.random.fold_in(streams_of[5], 71), 0),
        "token_keys": draw_token_keys(jax.random.fold_in(streams_of[5], 71), 0),
        "token_values": noise(streams_of[2], (TOKENS, HD), 1.0, 6.0, ((0, 32), (1, 4))),
        "out_weight": noise(streams_of[3], (HD, D), HD ** -0.5, 0.09375, ((0, 4),)),
        "out_grad": bell_draw_with(streams_of[4], (TOKENS, D), 1.0, 6.0, ((0, 32),), (0, 1, 32, 2.75)),
    }


def product(form, left, right):
    return jnp.einsum(form, left.astype(jnp.float32), right.astype(jnp.float32))

def pooled(stacked, group_size):
    count_rows = stacked.shape[1] // group_size
    summed = stacked.astype(jnp.float32).reshape(stacked.shape[0], count_rows, group_size, stacked.shape[2]).sum(axis=2)
    return (summed / group_size).astype(jnp.bfloat16)

def expand_rows(grad_parts, group_size):
    shaped = jnp.broadcast_to(grad_parts[:, :, None, :] / group_size, (grad_parts.shape[0], grad_parts.shape[1], group_size, grad_parts.shape[2]))
    return shaped.reshape(grad_parts.shape[0], grad_parts.shape[1] * group_size, grad_parts.shape[2])

def fold_windows(window_grad, blocks):
    leading = window_grad.shape[0]
    split_grad = window_grad.reshape(leading, blocks, 3, FB, -1)
    first_part = jnp.pad(split_grad[:, :, 0], ((0, 0), (0, 2), (0, 0), (0, 0)))
    middle = jnp.pad(split_grad[:, :, 1], ((0, 0), (1, 1), (0, 0), (0, 0)))
    last_part = jnp.pad(split_grad[:, :, 2], ((0, 0), (2, 0), (0, 0), (0, 0)))
    return (first_part + middle + last_part).reshape(leading, (blocks + 2) * FB, -1)

def attend(query_rows, extended, extended_pooled, coarse_rows, grad_rows, position, seq_count):
    tokens_here, features = query_rows.shape
    head_count = features // DH
    blocks = tokens_here // FB
    pooled_rows = extended_pooled.shape[1] // 3
    coarse_count = coarse_rows.shape[1]
    scaling = 1.0 / math.sqrt(DH)
    query_blocks = query_rows.reshape(blocks, FB, head_count, DH)
    token_blocks = extended.reshape(2, blocks + 2, FB, head_count, DH)
    windows = jnp.concatenate([token_blocks[:, offset:offset + blocks] for offset in range(3)], axis=2)
    coarse_all = jnp.concatenate([extended_pooled, coarse_rows], axis=1).reshape(2, 3 * pooled_rows + coarse_count, head_count, DH)
    block_ids = jnp.arange(blocks, dtype=jnp.int32)[:, None]
    window_rows = block_ids * FB + jnp.arange(3 * FB, dtype=jnp.int32)[None, :]
    first_dev = position == 0
    last_dev = position == seq_count - 1
    fine_mask = jnp.logical_not(jnp.logical_or(jnp.logical_and(window_rows < FB, first_dev), jnp.logical_and(window_rows >= tokens_here + FB, last_dev)))
    group_ids = jnp.arange(3 * pooled_rows, dtype=jnp.int32)
    group_dev = group_ids // pooled_rows
    present = jnp.logical_not(jnp.logical_or(jnp.logical_and(group_dev == 0, first_dev), jnp.logical_and(group_dev == 2, last_dev)))
    distance = group_ids[None, :] * P1 // FB - blocks - block_ids
    near_mask = jnp.logical_and(present[None, :], jnp.abs(distance) > 1)
    coarse_dev = jnp.arange(coarse_count, dtype=jnp.int32) * P2 // tokens_here
    far_mask = jnp.abs(coarse_dev - position) > 1
    coarse_mask = jnp.concatenate([near_mask, jnp.broadcast_to(far_mask[None, :], (blocks, coarse_count))], axis=1)
    level_bias = jnp.concatenate([jnp.full((3 * pooled_rows,), math.log(P1), jnp.float32), jnp.full((coarse_count,), math.log(P2), jnp.float32)])
    fine_scores = jnp.where(fine_mask[None, :, None, :], product('bqhd,bkhd->hbqk', query_blocks, windows[0]) * scaling, -jnp.inf)
    coarse_scores = jnp.where(coarse_mask[None, :, None, :], product('bqhd,khd->hbqk', query_blocks, coarse_all[0]) * scaling + level_bias, -jnp.inf)
    row_peak = jnp.maximum(fine_scores.max(axis=-1), coarse_scores.max(axis=-1))
    row_total = jnp.exp(fine_scores - row_peak[..., None]).sum(axis=-1) + jnp.exp(coarse_scores - row_peak[..., None]).sum(axis=-1)
    log_total = row_peak + jnp.log(row_total)
    fine_prob = jnp.exp(fine_scores - log_total[..., None])
    coarse_prob = jnp.exp(coarse_scores - log_total[..., None])
    fine_round = fine_prob.astype(jnp.bfloat16)
    coarse_round = coarse_prob.astype(jnp.bfloat16)
    attention = (product('hbqk,bkhd->bqhd', fine_round, windows[1]) + product('hbqk,khd->bqhd', coarse_round, coarse_all[1])).astype(jnp.bfloat16)
    grad_blocks = grad_rows.reshape(blocks, FB, head_count, DH)
    row_delta = product('bqhd,bqhd->hbq', grad_blocks, attention)
    fine_ds = (fine_prob * (product('bqhd,bkhd->hbqk', grad_blocks, windows[1]) - row_delta[..., None])).astype(jnp.bfloat16)
    coarse_ds = (coarse_prob * (product('bqhd,khd->hbqk', grad_blocks, coarse_all[1]) - row_delta[..., None])).astype(jnp.bfloat16)
    query_grad = ((product('hbqk,bkhd->bqhd', fine_ds, windows[0]) + product('hbqk,khd->bqhd', coarse_ds, coarse_all[0])) * scaling).astype(jnp.bfloat16)
    window_grad = jnp.stack([product('hbqk,bqhd->bkhd', fine_ds, query_blocks) * scaling, product('hbqk,bqhd->bkhd', fine_round, grad_blocks)])
    coarse_grad = jnp.stack([product('hbqk,bqhd->khd', coarse_ds, query_blocks) * scaling, product('hbqk,bqhd->khd', coarse_round, grad_blocks)])
    coarse_grad = coarse_grad.reshape(2, 3 * pooled_rows + coarse_count, features)
    extended_grad = fold_windows(window_grad.reshape(2, blocks, 3 * FB, features), blocks)
    return (attention.reshape(tokens_here, features), query_grad.reshape(tokens_here, features), extended_grad, coarse_grad[:, :3 * pooled_rows], coarse_grad[:, 3 * pooled_rows:])

def reference(queries, token_keys, token_values, out_weight, out_grad):
    features = HEADS * DH
    pooled_rows = TOK_DEV // P1
    stacked = jnp.stack([token_keys, token_values])
    fine_pad = jnp.pad(stacked, ((0, 0), (FB, FB), (0, 0)))
    near_rows = pooled(stacked, P1)
    near_pad = jnp.pad(near_rows, ((0, 0), (pooled_rows, pooled_rows), (0, 0)))
    far_rows = pooled(stacked, P2)
    attn_grad = lax.dot_general(out_grad, out_weight, (((1,), (1,)), ((), ())), preferred_element_type=jnp.float32).astype(jnp.bfloat16)
    anchor = jnp.zeros((), jnp.int32)

    def one_block(position):
        row_start = (position * TOK_DEV).astype(jnp.int32)
        query_rows = lax.dynamic_slice(queries, (row_start, anchor), (TOK_DEV, features))
        extended = lax.dynamic_slice(fine_pad, (anchor, row_start, anchor), (2, TOK_DEV + 2 * FB, features))
        extended_pooled = lax.dynamic_slice(near_pad, (anchor, (position * pooled_rows).astype(jnp.int32), anchor), (2, 3 * pooled_rows, features))
        grad_rows = lax.dynamic_slice(attn_grad, (row_start, anchor), (TOK_DEV, features))
        return attend(query_rows, extended, extended_pooled, far_rows, grad_rows, position, N_SEQ)
    attention, query_grad, window_grad, near_grad, far_grad = lax.map(one_block, jnp.arange(N_SEQ, dtype=jnp.int32))
    empty_fine = jnp.zeros_like(window_grad[:1, :, :FB])
    from_right = jnp.concatenate([window_grad[1:, :, :FB], empty_fine], axis=0)
    from_left = jnp.concatenate([empty_fine, window_grad[:-1, :, TOK_DEV + FB:]], axis=0)
    fine_total = window_grad[:, :, FB:FB + TOK_DEV] + jnp.pad(from_left, ((0, 0), (0, 0), (0, TOK_DEV - FB), (0, 0))) + jnp.pad(from_right, ((0, 0), (0, 0), (TOK_DEV - FB, 0), (0, 0)))
    empty_near = jnp.zeros_like(near_grad[:1, :, :pooled_rows])
    near_total = near_grad[:, :, pooled_rows:2 * pooled_rows] + jnp.concatenate([near_grad[1:, :, :pooled_rows], empty_near], axis=0) + jnp.concatenate([empty_near, near_grad[:-1, :, 2 * pooled_rows:]], axis=0)
    far_total = far_grad.sum(axis=0)
    fine_total = fine_total.transpose(1, 0, 2, 3).reshape(2, TOKENS, features)
    near_total = near_total.transpose(1, 0, 2, 3).reshape(2, TOKENS // P1, features)
    grand = fine_total + expand_rows(near_total, P1) + expand_rows(far_total, P2)
    attention = attention.reshape(TOKENS, features)
    query_grad = query_grad.reshape(TOKENS, features)
    layer_out = jnp.dot(attention, out_weight, preferred_element_type=jnp.float32).astype(jnp.bfloat16)
    weight_grad = jnp.dot(attention.T, out_grad, preferred_element_type=jnp.float32) * (1.0 / math.sqrt(TOKENS))
    return (layer_out, query_grad, grand[0].astype(jnp.bfloat16), grand[1].astype(jnp.bfloat16), weight_grad)
```

```python
import functools
import math

import jax
import jax.numpy as jnp
from jax import lax
from jax.experimental import pallas as pl
from jax.experimental.pallas import tpu as pltpu
from jax.sharding import PartitionSpec as P

DH = 128
FB = 128
P1 = 16
P2 = 256
BF = jnp.bfloat16
F32 = jnp.float32
NEG = -1e30
LOG2E = math.log2(math.e)
MB = 1024 * 1024


def dot(a, b, ca, cb):
    return lax.dot_general(a, b, (((ca,), (cb,)), ((), ())), preferred_element_type=F32)


def params(limit):
    return pltpu.CompilerParams(vmem_limit_bytes=limit * MB)


def pool_kernel(k_ref, v_ref, near_ref, far_ref, left_ref, right_ref):
    rows = k_ref.shape[0]
    for i, ref in enumerate((k_ref, v_ref)):
        x = ref[...].astype(F32)
        s16 = x.reshape(rows // P1, P1, x.shape[1]).sum(axis=1)
        near = (s16 * (1.0 / P1)).astype(BF)
        far = s16.reshape(rows // P2, P2 // P1, x.shape[1]).sum(axis=1) * (1.0 / P2)
        near_ref[i] = near
        far_ref[i] = far.astype(BF)
        left_ref[i, :FB] = ref[:FB]
        right_ref[i, :FB] = ref[rows - FB :]
        left_ref[i, FB:] = near
        right_ref[i, FB:] = near


def pool(k, v):
    rows, feats = k.shape
    nr, fr = rows // P1, rows // P2
    cols = 256
    blk = lambda r: pl.BlockSpec((2, r, cols), lambda j: (0, 0, j))
    out = lambda r: jax.ShapeDtypeStruct((2, r, feats), BF)
    return pl.pallas_call(
        pool_kernel,
        grid=(feats // cols,),
        in_specs=[pl.BlockSpec((rows, cols), lambda j: (0, j))] * 2,
        out_specs=[blk(nr), blk(fr), blk(FB + nr), blk(FB + nr)],
        out_shape=[out(nr), out(fr), out(FB + nr), out(FB + nr)],
        compiler_params=params(24),
        name="pool",
    )(k, v)


def level_bias(position, blocks, pooled_rows, coarse_count, tokens_here, seq_count):
    group_ids = jnp.arange(3 * pooled_rows, dtype=jnp.int32)
    group_dev = group_ids // pooled_rows
    absent = ((group_dev == 0) & (position == 0)) | ((group_dev == 2) & (position == seq_count - 1))
    block_ids = jnp.arange(blocks, dtype=jnp.int32)[:, None]
    distance = group_ids[None, :] * P1 // FB - blocks - block_ids
    near = jnp.where(absent[None, :] | (jnp.abs(distance) <= 1), NEG, math.log(P1) * LOG2E)
    coarse_dev = jnp.arange(coarse_count, dtype=jnp.int32) * P2 // tokens_here
    far = jnp.where(jnp.abs(coarse_dev - position) > 1, math.log(P2) * LOG2E, NEG)
    far = jnp.broadcast_to(far[None, :], (blocks, coarse_count))
    bias = jnp.concatenate([near, far], axis=1).astype(F32)
    return jnp.broadcast_to(bias[:, :, None], (*bias.shape, FB))


def gathered(i, left_ref, own_ref, right_ref, near_ref, far_ref):
    keys = jnp.concatenate([left_ref[i, :FB], own_ref[...], right_ref[i, :FB]], axis=0)
    coarse = jnp.concatenate([left_ref[i, FB:], near_ref[i], right_ref[i, FB:], far_ref[i]], axis=0)
    return keys, coarse


def scores(b, blocks, pos_ref, seq_count, q, keys, coarse_scores, bias_ref):
    scale = LOG2E / math.sqrt(DH)
    qb = q[b * FB : (b + 1) * FB]
    fine = dot(keys[b * FB : (b + 3) * FB], qb, 1, 1) * scale
    if b == 0:
        edge = jnp.where(pos_ref[0] == 0, NEG, 0.0).astype(F32)
        fine = jnp.concatenate([fine[:FB] + edge, fine[FB:]], axis=0)
    if b == blocks - 1:
        edge = jnp.where(pos_ref[0] == seq_count - 1, NEG, 0.0).astype(F32)
        fine = jnp.concatenate([fine[: 2 * FB], fine[2 * FB :] + edge], axis=0)
    coarse = coarse_scores[:, b * FB : (b + 1) * FB] * scale + bias_ref[b]
    return fine, coarse


def fwd_kernel(seq_count, pos_ref, q_ref, k_ref, v_ref, left_ref, right_ref, near_ref, far_ref, bias_ref, att_ref, attt_ref, lse_ref):
    blocks = q_ref.shape[0] // FB
    q = q_ref[...]
    keys, ckeys = gathered(0, left_ref, k_ref, right_ref, near_ref, far_ref)
    vals, cvals = gathered(1, left_ref, v_ref, right_ref, near_ref, far_ref)
    vals_t, cvals_t = vals.T, cvals.T
    csc = dot(ckeys, q, 1, 1)
    for b in range(blocks):
        fine, coarse = scores(b, blocks, pos_ref, seq_count, q, keys, csc, bias_ref)
        peak = jnp.maximum(fine.max(axis=0, keepdims=True), coarse.max(axis=0, keepdims=True))
        pf = jnp.exp2(fine - peak)
        pc = jnp.exp2(coarse - peak)
        total = pf.sum(axis=0, keepdims=True) + pc.sum(axis=0, keepdims=True)
        lse_ref[0, :, b * FB : (b + 1) * FB] = peak + jnp.log2(total)
        out_t = dot(vals_t[:, b * FB : (b + 3) * FB], pf.astype(BF), 1, 0) + dot(cvals_t, pc.astype(BF), 1, 0)
        out_t = (out_t * (1.0 / total)).astype(BF)
        attt_ref[:, b * FB : (b + 1) * FB] = out_t
        att_ref[b * FB : (b + 1) * FB, :] = out_t.T


def bwd_kernel(
    seq_count, pos_ref, q_ref, k_ref, v_ref, left_ref, right_ref, near_ref, far_ref, bias_ref, do_ref, att_ref, lse_ref,
    dq_ref, gk_ref, gv_ref, sl_ref, sr_ref, gfar_ref, p_ref, ds_ref, cp_ref, cds_ref,
):
    blocks = q_ref.shape[0] // FB
    own = blocks * FB
    inv = 1.0 / math.sqrt(DH)
    q, do = q_ref[...], do_ref[...]
    keys, ckeys = gathered(0, left_ref, k_ref, right_ref, near_ref, far_ref)
    vals, cvals = gathered(1, left_ref, v_ref, right_ref, near_ref, far_ref)
    keys_t, ckeys_t = keys.T, ckeys.T
    csc = dot(ckeys, q, 1, 1)
    cdp = dot(cvals, do, 1, 1)
    delta_all = (do.astype(F32) * att_ref[...].astype(F32)).T.sum(axis=0, keepdims=True)
    for b in range(blocks):
        cols = slice(b * FB, (b + 1) * FB)
        fine, coarse = scores(b, blocks, pos_ref, seq_count, q, keys, csc, bias_ref)
        lse = lse_ref[0, :, cols]
        delta = delta_all[:, cols]
        pf = jnp.exp2(fine - lse)
        pc = jnp.exp2(coarse - lse)
        dpf = dot(vals[b * FB : (b + 3) * FB], do[cols], 1, 1)
        dsf = (pf * (dpf - delta)).astype(BF)
        dsc = (pc * (cdp[:, cols] - delta)).astype(BF)
        p_ref[b * FB : (b + 3) * FB, cols] = pf.astype(BF)
        ds_ref[b * FB : (b + 3) * FB, cols] = dsf
        cp_ref[:, cols] = pc.astype(BF)
        cds_ref[:, cols] = dsc
        dq_t = dot(keys_t[:, b * FB : (b + 3) * FB], dsf, 1, 0) + dot(ckeys_t, dsc, 1, 0)
        dq_ref[cols, :] = (dq_t * inv).astype(BF).T
    nr = near_ref.shape[1]
    for i, (src, csrc, rhs, mul, g_ref) in enumerate(((ds_ref, cds_ref, q, inv, gk_ref), (p_ref, cp_ref, do, 1.0, gv_ref))):
        cg = dot(csrc[...], rhs, 1, 0) * mul
        sl_ref[i, FB:] = cg[:nr].astype(BF)
        sr_ref[i, FB:] = cg[2 * nr : 3 * nr].astype(BF)
        gfar_ref[i] = cg[3 * nr :]
        mine = cg[nr : 2 * nr] * (1.0 / P1)
        for c in range(blocks + 2):
            lo, hi = max(0, c - 2), min(blocks, c + 1)
            part = dot(src[c * FB : (c + 1) * FB, lo * FB : hi * FB], rhs[lo * FB : hi * FB], 1, 0) * mul
            if c == 0:
                sl_ref[i, :FB] = part.astype(BF)
            elif c == blocks + 1:
                sr_ref[i, :FB] = part.astype(BF)
            else:
                r = c - 1
                per = FB // P1
                spread = jnp.broadcast_to(mine[r * per : (r + 1) * per, None, :], (per, P1, DH)).reshape(FB, DH)
                g_ref[r * FB : (r + 1) * FB, :] = part + spread


def attention_specs(tokens, halo, nr, fr, blocks):
    tok = pl.BlockSpec((tokens, DH), lambda h, *_: (0, h))
    lev = lambda r: pl.BlockSpec((2, r, DH), lambda h, *_: (0, 0, h))
    bias = pl.BlockSpec((blocks, 3 * nr + fr, FB), lambda h, *_: (0, 0, 0))
    return tok, [tok, tok, tok, lev(halo), lev(halo), lev(nr), lev(fr), bias], lev


def forward(seq_count, pos, q, k, v, left, right, near, far, bias):
    tokens, feats = q.shape
    heads = feats // DH
    tok, specs, _ = attention_specs(tokens, left.shape[1], near.shape[1], far.shape[1], tokens // FB)
    return pl.pallas_call(
        functools.partial(fwd_kernel, seq_count),
        grid_spec=pltpu.PrefetchScalarGridSpec(
            num_scalar_prefetch=1,
            grid=(heads,),
            in_specs=specs,
            out_specs=[tok, pl.BlockSpec((DH, tokens), lambda h, *_: (h, 0)), pl.BlockSpec((1, 1, tokens), lambda h, *_: (h, 0, 0))],
        ),
        out_shape=[
            jax.ShapeDtypeStruct((tokens, feats), BF),
            jax.ShapeDtypeStruct((feats, tokens), BF),
            jax.ShapeDtypeStruct((heads, 1, tokens), F32),
        ],
        compiler_params=params(32),
        name="attend",
    )(pos, q, k, v, left, right, near, far, bias)


def backward(seq_count, pos, q, k, v, left, right, near, far, bias, do, att, lse):
    tokens, feats = q.shape
    heads = feats // DH
    halo, nr, fr = left.shape[1], near.shape[1], far.shape[1]
    tok, specs, lev = attention_specs(tokens, halo, nr, fr, tokens // FB)
    coarse = 3 * nr + fr
    return pl.pallas_call(
        functools.partial(bwd_kernel, seq_count),
        grid_spec=pltpu.PrefetchScalarGridSpec(
            num_scalar_prefetch=1,
            grid=(heads,),
            in_specs=[*specs, tok, tok, pl.BlockSpec((1, 1, tokens), lambda h, *_: (h, 0, 0))],
            out_specs=[tok, tok, tok, lev(halo), lev(halo), lev(fr)],
            scratch_shapes=[
                pltpu.VMEM((tokens + 2 * FB, tokens), BF),
                pltpu.VMEM((tokens + 2 * FB, tokens), BF),
                pltpu.VMEM((coarse, tokens), BF),
                pltpu.VMEM((coarse, tokens), BF),
            ],
        ),
        out_shape=[
            jax.ShapeDtypeStruct((tokens, feats), BF),
            jax.ShapeDtypeStruct((tokens, feats), F32),
            jax.ShapeDtypeStruct((tokens, feats), F32),
            jax.ShapeDtypeStruct((2, halo, feats), BF),
            jax.ShapeDtypeStruct((2, halo, feats), BF),
            jax.ShapeDtypeStruct((2, fr, feats), F32),
        ],
        compiler_params=params(40),
        name="attend_grad",
    )(pos, q, k, v, left, right, near, far, bias, do, att, lse)


def combine_kernel(gk_ref, gv_ref, left_ref, right_ref, far_ref, ok_ref, ov_ref):
    rows, width = gk_ref.shape
    for i, (g_ref, o_ref) in enumerate(((gk_ref, ok_ref), (gv_ref, ov_ref))):
        near = (left_ref[i, FB:].astype(F32) + right_ref[i, FB:].astype(F32)) * (1.0 / P1)
        per = FB // P1
        for r in range(rows // FB):
            part = g_ref[r * FB : (r + 1) * FB]
            part += jnp.broadcast_to(near[r * per : (r + 1) * per, None, :], (per, P1, width)).reshape(FB, width)
            g = r * FB // P2
            part += far_ref[i, g : g + 1] * (1.0 / P2)
            if r == 0:
                part += left_ref[i, :FB].astype(F32)
            if r == rows // FB - 1:
                part += right_ref[i, :FB].astype(F32)
            o_ref[r * FB : (r + 1) * FB] = part.astype(BF)


def combine(gk, gv, from_left, from_right, far):
    rows, feats = gk.shape
    cols = 256
    tok = pl.BlockSpec((rows, cols), lambda j: (0, j))
    lev = lambda r: pl.BlockSpec((2, r, cols), lambda j: (0, 0, j))
    halo = from_left.shape[1]
    return pl.pallas_call(
        combine_kernel,
        grid=(feats // cols,),
        in_specs=[tok, tok, lev(halo), lev(halo), lev(far.shape[1])],
        out_specs=[tok, tok],
        out_shape=[jax.ShapeDtypeStruct((rows, feats), BF)] * 2,
        compiler_params=params(32),
        name="combine",
    )(gk, gv, from_left, from_right, far)


UNITS = 4
ROUTE = ((0, 1, 3), (0, 3, 1), (1, 1, 3), (1, 3, 1))


def weight_kernel(cols_ref, attt_ref, og_ref, *out_refs):
    j = pl.program_id(0)
    width = out_refs[0].shape[-1]
    rows = attt_ref.shape[0] // UNITS
    for u, o_ref in enumerate(out_refs):
        at = pl.multiple_of(cols_ref[u, j] * (2 * width), 2 * width)
        res = dot(attt_ref[u * rows : (u + 1) * rows, :], og_ref[:, pl.ds(at, 2 * width)], 1, 0).astype(BF)
        o_ref[0, 0] = res[:, :width]
        o_ref[0, 1] = res[:, width:]


def weight_parts(cols, attt, og, width):
    feats, tokens = attt.shape
    steps = cols.shape[1]
    rows = feats // UNITS
    whole = lambda a: pl.BlockSpec(a.shape, lambda j, *_: (0, 0))
    return pl.pallas_call(
        weight_kernel,
        grid_spec=pltpu.PrefetchScalarGridSpec(
            num_scalar_prefetch=1,
            grid=(steps,),
            in_specs=[whole(attt), whole(og)],
            out_specs=[pl.BlockSpec((1, 2, rows, width), lambda j, *_: (j, 0, 0, 0))] * UNITS,
        ),
        out_shape=[jax.ShapeDtypeStruct((steps, 2, rows, width), BF)] * UNITS,
        compiler_params=params(40),
        name="weight_parts",
    )(cols, attt, og)


def layer_kernel(cols_ref, att_ref, w_ref, o_ref):
    o_ref[0] = dot(att_ref[...], w_ref[...], 1, 0).astype(BF)


def layer_parts(cols, att, w, width):
    tokens, feats = att.shape
    steps = cols.shape[0]
    sub = 2
    n = width // sub
    return pl.pallas_call(
        layer_kernel,
        grid_spec=pltpu.PrefetchScalarGridSpec(
            num_scalar_prefetch=1,
            grid=(steps, sub),
            in_specs=[
                pl.BlockSpec((tokens, feats), lambda j, s, *_: (0, 0)),
                pl.BlockSpec((feats, n), lambda j, s, c: (0, c[j] * sub + s)),
            ],
            out_specs=pl.BlockSpec((1, tokens, n), lambda j, s, *_: (j, 0, s)),
        ),
        out_shape=jax.ShapeDtypeStruct((steps, tokens, width), BF),
        compiler_params=params(40),
        name="layer_parts",
    )(cols, att, w)


def swap(x, axis, bits):
    n = lax.axis_size(axis)
    return lax.ppermute(x, axis, [(i, i ^ bits) for i in range(n)])


def add(a, b):
    return (a.astype(F32) + b.astype(F32)).astype(BF)


def shards(queries, token_keys, token_values, out_weight, out_grad):
    pos = lax.axis_index("seq").astype(jnp.int32)
    tp = lax.axis_index("tp").astype(jnp.int32)
    seq_count, tp_count = lax.axis_size("seq"), lax.axis_size("tp")
    tokens, feats = queries.shape
    width = out_weight.shape[1]
    pos1 = pos[None]
    right_perm = [(i, i + 1) for i in range(seq_count - 1)]
    left_perm = [(i + 1, i) for i in range(seq_count - 1)]

    near, far_own, to_left, to_right = pool(token_keys, token_values)
    from_left = lax.ppermute(to_right, "seq", right_perm)
    from_right = lax.ppermute(to_left, "seq", left_perm)
    far = lax.all_gather(far_own, "seq", axis=1, tiled=True)
    attn_grad = dot(out_grad, out_weight, 1, 1).astype(BF)
    bias = level_bias(pos, tokens // FB, near.shape[1], far.shape[1], tokens, seq_count)
    args = (seq_count, pos1, queries, token_keys, token_values, from_left, from_right, near, far, bias)
    att, attt, lse = forward(*args)

    part = width // seq_count
    shift = (3, 1)
    coord = ((pos >> 3) & 3, (pos >> 1) & 3)
    rows = []
    for axis, k1, k2 in ROUTE:
        rel = jnp.array([0, k2, k1, k1 ^ k2], jnp.int32)
        first = coord[axis] ^ rel
        second = coord[1 - axis] ^ rel
        xs, ys = (first[:, None], second[None, :]) if axis == 0 else (second[None, :], first[:, None])
        rows.append((xs * 4 + ys).reshape(-1))
    cols = jnp.stack(rows).astype(jnp.int32)
    send = weight_parts(cols[:, 8:], attt, out_grad, part)
    got = [swap(s, "seq", k1 << shift[axis]) for s, (axis, k1, k2) in zip(send, ROUTE)]
    keep = weight_parts(cols[:, :8], attt, out_grad, part)

    c, zl = tp & 1, tp >> 1
    mine = jnp.stack([zl, zl ^ 1]) * 2
    lwidth = width // tp_count
    lsend = layer_parts(mine + (c ^ 1), att, out_weight, lwidth)
    lgot = swap(lsend, "tp", 1)
    lkeep = layer_parts(mine + c, att, out_weight, lwidth)
    lgot2 = swap(add(lkeep[1], lgot[1]), "tp", 2)
    layer_out = (lkeep[0].astype(F32) + lgot[0].astype(F32) + lgot2.astype(F32)).astype(BF)

    dq, gk, gv, sl, sr, gfar = backward(*args, attn_grad, att, lse)
    back_left = lax.ppermute(sr, "seq", right_perm)
    back_right = lax.ppermute(sl, "seq", left_perm)
    far_sum = lax.psum_scatter(gfar, "seq", scatter_dimension=1, tiled=True)

    nxt = []
    for k, r, (axis, k1, k2) in zip(keep, got, ROUTE):
        s2 = add(k[4:], r[4:])
        nxt.append((add(k[:4], r[:4]), swap(s2, "seq", k2 << shift[axis])))
    halves = []
    for p in (0, 2):
        axis = ROUTE[p][0]
        a = [add(k, r) for k, r in nxt[p : p + 2]]
        outs = []
        for unit, x in zip(ROUTE[p : p + 2], a):
            _, k1, k2 = unit
            o = shift[1 - axis]
            x = add(x[:2], swap(x[2:], "seq", k1 << o))
            x = add(x[:1], swap(x[1:], "seq", k2 << o))
            outs.append(x[0])
        halves.append(jnp.concatenate(outs, axis=1))
    wsum = jnp.concatenate(halves, axis=1)
    zh = pos & 1
    wkeep = lax.dynamic_index_in_dim(wsum, zh, 0, keepdims=False)
    wsend = lax.dynamic_index_in_dim(wsum, zh ^ 1, 0, keepdims=False)
    wgot = swap(wsend, "seq", 1)
    weight_grad = (wkeep.astype(F32) + wgot.astype(F32)) * (1.0 / math.sqrt(tokens * seq_count))

    key_grad, value_grad = combine(gk, gv, back_left, back_right, far_sum)
    return layer_out, dq, key_grad, value_grad, weight_grad


def solution(mesh):
    return jax.shard_map(
        shards,
        mesh=mesh,
        in_specs=(P("seq", "tp"), P("seq", "tp"), P("seq", "tp"), P("tp", None), P("seq", None)),
        out_specs=(P("seq", "tp"), P("seq", "tp"), P("seq", "tp"), P("seq", "tp"), P("tp", "seq")),
        check_vma=False,
    )
```

```python
import functools
import math

import jax
import jax.numpy as jnp
from jax import lax
from jax.experimental import pallas as pl
from jax.experimental.pallas import tpu as pltpu
from jax.sharding import PartitionSpec as P

DH = 128
FB = 128
P1 = 16
P2 = 256
BF = jnp.bfloat16
F32 = jnp.float32
NEG = -1e30
LOG2E = math.log2(math.e)
MB = 1024 * 1024
HALVES = 2
BIG = 58


def dot(a, b, ca, cb):
    return lax.dot_general(a, b, (((ca,), (cb,)), ((), ())), preferred_element_type=F32)


def params(limit):
    return pltpu.CompilerParams(vmem_limit_bytes=limit * MB)


def pool_kernel(k_ref, v_ref, near_ref, far_ref, left_ref, right_ref):
    rows = k_ref.shape[0]
    for i, ref in enumerate((k_ref, v_ref)):
        x = ref[...].astype(F32)
        s16 = x.reshape(rows // P1, P1, x.shape[1]).sum(axis=1)
        near = (s16 * (1.0 / P1)).astype(BF)
        far = s16.reshape(rows // P2, P2 // P1, x.shape[1]).sum(axis=1) * (1.0 / P2)
        near_ref[i] = near
        far_ref[i] = far.astype(BF)
        left_ref[i, :FB] = ref[:FB]
        right_ref[i, :FB] = ref[rows - FB :]
        left_ref[i, FB:] = near
        right_ref[i, FB:] = near


def pool(k, v, half):
    rows, feats = k.shape[0], k.shape[1] // HALVES
    nr, fr = rows // P1, rows // P2
    cols = 256
    per = feats // cols
    blk = lambda r: pl.BlockSpec((2, r, cols), lambda j: (0, 0, j))
    out = lambda r: jax.ShapeDtypeStruct((2, r, feats), BF)
    return pl.pallas_call(
        pool_kernel,
        grid=(per,),
        in_specs=[pl.BlockSpec((rows, cols), lambda j: (0, half * per + j))] * 2,
        out_specs=[blk(nr), blk(fr), blk(FB + nr), blk(FB + nr)],
        out_shape=[out(nr), out(fr), out(FB + nr), out(FB + nr)],
        compiler_params=params(BIG),
        name="pool",
    )(k, v)


def level_bias(position, blocks, pooled_rows, coarse_count, tokens_here, seq_count):
    group_ids = jnp.arange(3 * pooled_rows, dtype=jnp.int32)
    group_dev = group_ids // pooled_rows
    absent = ((group_dev == 0) & (position == 0)) | ((group_dev == 2) & (position == seq_count - 1))
    block_ids = jnp.arange(blocks, dtype=jnp.int32)[:, None]
    distance = group_ids[None, :] * P1 // FB - blocks - block_ids
    near = jnp.where(absent[None, :] | (jnp.abs(distance) <= 1), NEG, math.log(P1) * LOG2E)
    coarse_dev = jnp.arange(coarse_count, dtype=jnp.int32) * P2 // tokens_here
    far = jnp.where(jnp.abs(coarse_dev - position) > 1, math.log(P2) * LOG2E, NEG)
    far = jnp.broadcast_to(far[None, :], (blocks, coarse_count))
    bias = jnp.concatenate([near, far], axis=1).astype(F32)
    return jnp.broadcast_to(bias[:, :, None], (*bias.shape, FB))


def gathered(i, left_ref, own_ref, right_ref, near_ref, far_ref):
    keys = jnp.concatenate([left_ref[i, :FB], own_ref[...], right_ref[i, :FB]], axis=0)
    coarse = jnp.concatenate([left_ref[i, FB:], near_ref[i], right_ref[i, FB:], far_ref[i]], axis=0)
    return keys, coarse


def scores(b, blocks, pos_ref, seq_count, q, keys, coarse_scores, bias_ref):
    scale = LOG2E / math.sqrt(DH)
    qb = q[b * FB : (b + 1) * FB]
    fine = dot(keys[b * FB : (b + 3) * FB], qb, 1, 1) * scale
    if b == 0:
        edge = jnp.where(pos_ref[0] == 0, NEG, 0.0).astype(F32)
        fine = jnp.concatenate([fine[:FB] + edge, fine[FB:]], axis=0)
    if b == blocks - 1:
        edge = jnp.where(pos_ref[0] == seq_count - 1, NEG, 0.0).astype(F32)
        fine = jnp.concatenate([fine[: 2 * FB], fine[2 * FB :] + edge], axis=0)
    coarse = coarse_scores[:, b * FB : (b + 1) * FB] * scale + bias_ref[b]
    return fine, coarse


def fwd_kernel(seq_count, pos_ref, q_ref, k_ref, v_ref, left_ref, right_ref, near_ref, far_ref, bias_ref, att_ref, attt_ref, lse_ref):
    blocks = q_ref.shape[0] // FB
    q = q_ref[...]
    keys, ckeys = gathered(0, left_ref, k_ref, right_ref, near_ref, far_ref)
    vals, cvals = gathered(1, left_ref, v_ref, right_ref, near_ref, far_ref)
    vals_t, cvals_t = vals.T, cvals.T
    csc = dot(ckeys, q, 1, 1)
    for b in range(blocks):
        fine, coarse = scores(b, blocks, pos_ref, seq_count, q, keys, csc, bias_ref)
        peak = jnp.maximum(fine.max(axis=0, keepdims=True), coarse.max(axis=0, keepdims=True))
        pf = jnp.exp2(fine - peak)
        pc = jnp.exp2(coarse - peak)
        total = pf.sum(axis=0, keepdims=True) + pc.sum(axis=0, keepdims=True)
        lse_ref[0, :, b * FB : (b + 1) * FB] = peak + jnp.log2(total)
        out_t = dot(vals_t[:, b * FB : (b + 3) * FB], pf.astype(BF), 1, 0) + dot(cvals_t, pc.astype(BF), 1, 0)
        out_t = (out_t * (1.0 / total)).astype(BF)
        attt_ref[:, b * FB : (b + 1) * FB] = out_t
        att_ref[b * FB : (b + 1) * FB, :] = out_t.T


def bwd_kernel(
    seq_count, pos_ref, q_ref, k_ref, v_ref, left_ref, right_ref, near_ref, far_ref, bias_ref, do_ref, att_ref, lse_ref,
    dq_ref, gk_ref, gv_ref, sl_ref, sr_ref, gfar_ref, p_ref, ds_ref, cp_ref, cds_ref,
):
    blocks = q_ref.shape[0] // FB
    own = blocks * FB
    inv = 1.0 / math.sqrt(DH)
    q, do = q_ref[...], do_ref[...]
    keys, ckeys = gathered(0, left_ref, k_ref, right_ref, near_ref, far_ref)
    vals, cvals = gathered(1, left_ref, v_ref, right_ref, near_ref, far_ref)
    keys_t, ckeys_t = keys.T, ckeys.T
    csc = dot(ckeys, q, 1, 1)
    cdp = dot(cvals, do, 1, 1)
    delta_all = (do.astype(F32) * att_ref[...].astype(F32)).T.sum(axis=0, keepdims=True)
    for b in range(blocks):
        cols = slice(b * FB, (b + 1) * FB)
        fine, coarse = scores(b, blocks, pos_ref, seq_count, q, keys, csc, bias_ref)
        lse = lse_ref[0, :, cols]
        delta = delta_all[:, cols]
        pf = jnp.exp2(fine - lse)
        pc = jnp.exp2(coarse - lse)
        dpf = dot(vals[b * FB : (b + 3) * FB], do[cols], 1, 1)
        dsf = (pf * (dpf - delta)).astype(BF)
        dsc = (pc * (cdp[:, cols] - delta)).astype(BF)
        p_ref[b * FB : (b + 3) * FB, cols] = pf.astype(BF)
        ds_ref[b * FB : (b + 3) * FB, cols] = dsf
        cp_ref[:, cols] = pc.astype(BF)
        cds_ref[:, cols] = dsc
        dq_t = dot(keys_t[:, b * FB : (b + 3) * FB], dsf, 1, 0) + dot(ckeys_t, dsc, 1, 0)
        dq_ref[cols, :] = (dq_t * inv).astype(BF).T
    nr = near_ref.shape[1]
    for i, (src, csrc, rhs, mul, g_ref) in enumerate(((ds_ref, cds_ref, q, inv, gk_ref), (p_ref, cp_ref, do, 1.0, gv_ref))):
        cg = dot(csrc[...], rhs, 1, 0) * mul
        sl_ref[i, FB:] = cg[:nr].astype(BF)
        sr_ref[i, FB:] = cg[2 * nr : 3 * nr].astype(BF)
        gfar_ref[i] = cg[3 * nr :].astype(BF)
        mine = cg[nr : 2 * nr] * (1.0 / P1)
        for c in range(blocks + 2):
            lo, hi = max(0, c - 2), min(blocks, c + 1)
            part = dot(src[c * FB : (c + 1) * FB, lo * FB : hi * FB], rhs[lo * FB : hi * FB], 1, 0) * mul
            if c == 0:
                sl_ref[i, :FB] = part.astype(BF)
            elif c == blocks + 1:
                sr_ref[i, :FB] = part.astype(BF)
            else:
                r = c - 1
                per = FB // P1
                spread = jnp.broadcast_to(mine[r * per : (r + 1) * per, None, :], (per, P1, DH)).reshape(FB, DH)
                g_ref[r * FB : (r + 1) * FB, :] = part + spread


def forward(seq_count, pos, q, k, v, left, right, near, far, bias, half):
    tokens, feats = q.shape[0], q.shape[1] // HALVES
    heads, blocks = feats // DH, tokens // FB
    tok = pl.BlockSpec((tokens, DH), lambda h, *_: (0, half * heads + h))
    lev = lambda a: pl.BlockSpec((2, a.shape[1], DH), lambda h, *_: (0, 0, h))
    far_spec = pl.BlockSpec((2, far.shape[1], DH), lambda h, *_: (0, 0, half * heads + h))
    bias_spec = pl.BlockSpec(bias.shape, lambda h, *_: (0, 0, 0))
    return pl.pallas_call(
        functools.partial(fwd_kernel, seq_count),
        grid_spec=pltpu.PrefetchScalarGridSpec(
            num_scalar_prefetch=1,
            grid=(heads,),
            in_specs=[tok, tok, tok, lev(left), lev(right), lev(near), far_spec, bias_spec],
            out_specs=[
                pl.BlockSpec((tokens, DH), lambda h, *_: (0, h)),
                pl.BlockSpec((DH, tokens), lambda h, *_: (h, 0)),
                pl.BlockSpec((1, 1, tokens), lambda h, *_: (h, 0, 0)),
            ],
        ),
        out_shape=[
            jax.ShapeDtypeStruct((tokens, feats), BF),
            jax.ShapeDtypeStruct((feats, tokens), BF),
            jax.ShapeDtypeStruct((heads, 1, tokens), F32),
        ],
        compiler_params=params(BIG),
        name="attend",
    )(pos, q, k, v, left, right, near, far, bias)


def bwd_halves_kernel(seq_count, pos_ref, q_ref, k_ref, v_ref, *refs):
    per = pl.num_programs(0) // HALVES
    first = pl.program_id(0) < per
    pairs, rest = refs[: 5 * HALVES], refs[5 * HALVES :]
    picked = [jnp.where(first, pairs[2 * i][...], pairs[2 * i + 1][...]) for i in range(5)]
    left, right, near, att, lse = picked
    far_ref, bias_ref, do_ref, *outs = rest
    bwd_kernel(seq_count, pos_ref, q_ref, k_ref, v_ref, left, right, near, far_ref, bias_ref, do_ref, att, lse, *outs)


def backward(seq_count, pos, q, k, v, left, right, near, far, bias, do, att, lse):
    tokens, feats = q.shape
    heads = feats // DH
    per = heads // HALVES
    halo, nr, fr = left[0].shape[1], near[0].shape[1], far.shape[1]
    coarse = 3 * nr + fr
    tok = pl.BlockSpec((tokens, DH), lambda h, *_: (0, h))
    lev = lambda r: pl.BlockSpec((2, r, DH), lambda h, *_: (0, 0, h))
    at = (lambda h: jnp.minimum(h, per - 1), lambda h: jnp.maximum(h - per, 0))
    pairs, pair_specs = [], []
    for x in (left, right, near, att, lse):
        for half, pick in enumerate(at):
            pairs.append(x[half])
            if x is att:
                pair_specs.append(pl.BlockSpec((tokens, DH), lambda h, *_, p=pick: (0, p(h))))
            elif x is lse:
                pair_specs.append(pl.BlockSpec((1, 1, tokens), lambda h, *_, p=pick: (p(h), 0, 0)))
            else:
                pair_specs.append(pl.BlockSpec((2, x[half].shape[1], DH), lambda h, *_, p=pick: (0, 0, p(h))))
    return pl.pallas_call(
        functools.partial(bwd_halves_kernel, seq_count),
        grid_spec=pltpu.PrefetchScalarGridSpec(
            num_scalar_prefetch=1,
            grid=(heads,),
            in_specs=[tok, tok, tok, *pair_specs, lev(fr), pl.BlockSpec(bias.shape, lambda h, *_: (0, 0, 0)), tok],
            out_specs=[tok, tok, tok, lev(halo), lev(halo), lev(fr)],
            scratch_shapes=[
                pltpu.VMEM((tokens + 2 * FB, tokens), BF),
                pltpu.VMEM((tokens + 2 * FB, tokens), BF),
                pltpu.VMEM((coarse, tokens), BF),
                pltpu.VMEM((coarse, tokens), BF),
            ],
        ),
        out_shape=[
            jax.ShapeDtypeStruct((tokens, feats), BF),
            jax.ShapeDtypeStruct((tokens, feats), F32),
            jax.ShapeDtypeStruct((tokens, feats), F32),
            jax.ShapeDtypeStruct((2, halo, feats), BF),
            jax.ShapeDtypeStruct((2, halo, feats), BF),
            jax.ShapeDtypeStruct((2, fr, feats), BF),
        ],
        compiler_params=params(BIG),
        name="attend_grad",
    )(pos, q, k, v, *pairs, far, bias, do)


def combine_kernel(gk_ref, gv_ref, left_ref, right_ref, far_ref, ok_ref, ov_ref):
    rows, width = gk_ref.shape
    for i, (g_ref, o_ref) in enumerate(((gk_ref, ok_ref), (gv_ref, ov_ref))):
        near = (left_ref[i, FB:].astype(F32) + right_ref[i, FB:].astype(F32)) * (1.0 / P1)
        per = FB // P1
        for r in range(rows // FB):
            part = g_ref[r * FB : (r + 1) * FB]
            part += jnp.broadcast_to(near[r * per : (r + 1) * per, None, :], (per, P1, width)).reshape(FB, width)
            g = r * FB // P2
            part += far_ref[i, g : g + 1] * (1.0 / P2)
            if r == 0:
                part += left_ref[i, :FB].astype(F32)
            if r == rows // FB - 1:
                part += right_ref[i, :FB].astype(F32)
            o_ref[r * FB : (r + 1) * FB] = part.astype(BF)


def combine(gk, gv, from_left, from_right, far):
    rows, feats = gk.shape
    cols = 256
    tok = pl.BlockSpec((rows, cols), lambda j: (0, j))
    lev = lambda r: pl.BlockSpec((2, r, cols), lambda j: (0, 0, j))
    halo = from_left.shape[1]
    return pl.pallas_call(
        combine_kernel,
        grid=(feats // cols,),
        in_specs=[tok, tok, lev(halo), lev(halo), lev(far.shape[1])],
        out_specs=[tok, tok],
        out_shape=[jax.ShapeDtypeStruct((rows, feats), BF)] * 2,
        compiler_params=params(BIG),
        name="combine",
    )(gk, gv, from_left, from_right, far)


UNITS = 4
ROUTE = ((0, 1, 3), (0, 3, 1), (1, 1, 3), (1, 3, 1))
SECOND = ((1, 3), (3, 1))
SHIFT = (3, 1)


def block_order(pos):
    coord = ((pos >> 3) & 3, (pos >> 1) & 3)
    rows = []
    for u, (axis, k1, k2) in enumerate(ROUTE):
        m1, m2 = SECOND[u // 2]
        first = coord[axis] ^ jnp.array([0, k2, k1, k1 ^ k2], jnp.int32)
        second = coord[1 - axis] ^ jnp.array([0, m2, m1, m1 ^ m2], jnp.int32)
        at = first[:, None] * 4 + second[None, :] if axis == 0 else second[None, :] * 4 + first[:, None]
        rows.append(at.reshape(-1))
    return jnp.stack(rows).astype(jnp.int32)


def weight_kernel(n_units, n_recv, pair_out, cols_ref, *refs):
    atts, ogs = refs[:n_units], refs[n_units : 2 * n_units]
    recvs = refs[2 * n_units : 2 * n_units + n_recv]
    outs = refs[2 * n_units + n_recv :]
    for u in range(n_units):
        res = dot(atts[u][...], ogs[u][...], 1, 0)
        rows, width = res.shape[0], res.shape[1] // 2
        for z in range(2):
            part = res[:, z * width : (z + 1) * width]
            for r in recvs[u::n_units]:
                part += r[0, z].astype(F32)
            if pair_out:
                outs[u // 2][0, z, (u % 2) * rows : (u % 2 + 1) * rows] = part.astype(BF)
            else:
                outs[u][0, z] = part.astype(BF)


def weight_step(cols, attt, og, width, units, start, count, recvs, pair_out):
    tokens = attt[0].shape[1]
    rows = attt[0].shape[0] * HALVES // UNITS
    n = len(units)
    per_half = UNITS // HALVES
    in_specs, args = [], []
    for u in units:
        in_specs.append(pl.BlockSpec((rows, tokens), lambda j, *_, u=u: (u % per_half, 0)))
        args.append(attt[u // per_half])
    for u in units:
        in_specs.append(pl.BlockSpec((tokens, 2 * width), lambda j, c, u=u: (0, c[u, start + j])))
        args.append(og)
    for step in recvs:
        for u in units:
            r, paired = step[u]
            if paired:
                in_specs.append(pl.BlockSpec((1, 2, rows, width), lambda j, *_, u=u: (start + j, 0, u % 2, 0)))
            else:
                in_specs.append(pl.BlockSpec((1, 2, rows, width), lambda j, *_: (start + j, 0, 0, 0)))
            args.append(r)
    n_out = n // 2 if pair_out else n
    out_rows = 2 * rows if pair_out else rows
    return pl.pallas_call(
        functools.partial(weight_kernel, n, len(recvs) * n, pair_out),
        grid_spec=pltpu.PrefetchScalarGridSpec(
            num_scalar_prefetch=1,
            grid=(count,),
            in_specs=in_specs,
            out_specs=[pl.BlockSpec((1, 2, out_rows, width), lambda j, *_: (j, 0, 0, 0))] * n_out,
        ),
        out_shape=[jax.ShapeDtypeStruct((count, 2, out_rows, width), BF)] * n_out,
        compiler_params=params(BIG),
        name="weight_step",
    )(cols, *args)


def weight_last_kernel(scale, n_recv, last, cols_ref, *refs):
    o_ref = refs[-1]
    atts, ogs = refs[:UNITS], refs[UNITS : 2 * UNITS]
    recvs = refs[2 * UNITS : 2 * UNITS + n_recv]
    rows = atts[0].shape[0]
    for u in range(UNITS):
        part = dot(atts[u][...], ogs[u][...], 1, 0)
        for r in recvs[u::UNITS]:
            part += r[0, 0].astype(F32)
        if last:
            part += refs[2 * UNITS + n_recv][u * rows : (u + 1) * rows].astype(F32)
        o_ref[u * rows : (u + 1) * rows] = (part * scale).astype(o_ref.dtype)


def weight_last(cols, attt, og, width, z, recvs, got, scale, dtype):
    tokens = attt[0].shape[1]
    rows = attt[0].shape[0] * HALVES // UNITS
    per_half = UNITS // HALVES
    table = jnp.concatenate([cols[:, 0] * 2 + z, z[None]])
    in_specs, args = [], []
    for u in range(UNITS):
        in_specs.append(pl.BlockSpec((rows, tokens), lambda j, *_, u=u: (u % per_half, 0)))
        args.append(attt[u // per_half])
    for u in range(UNITS):
        in_specs.append(pl.BlockSpec((tokens, width), lambda j, c, u=u: (0, c[u])))
        args.append(og)
    for step in recvs:
        for u in range(UNITS):
            r, paired = step[u]
            at = u % 2 if paired else 0
            in_specs.append(pl.BlockSpec((1, 1, rows, width), lambda j, c, at=at: (0, c[UNITS], at, 0)))
            args.append(r)
    full = pl.BlockSpec((UNITS * rows, width), lambda j, *_: (0, 0))
    if got is not None:
        in_specs.append(full)
        args.append(got)
    return pl.pallas_call(
        functools.partial(weight_last_kernel, scale, len(recvs) * UNITS, got is not None),
        grid_spec=pltpu.PrefetchScalarGridSpec(num_scalar_prefetch=1, grid=(1,), in_specs=in_specs, out_specs=full),
        out_shape=jax.ShapeDtypeStruct((UNITS * rows, width), dtype),
        compiler_params=params(BIG),
        name="weight_last",
    )(table, *args)


def layer_kernel(cols_ref, a0_ref, a1_ref, w_ref, *refs):
    o_ref = refs[-1]
    half = a0_ref.shape[1]
    res = dot(a0_ref[...], w_ref[:half], 1, 0) + dot(a1_ref[...], w_ref[half:], 1, 0)
    for r in refs[:-1]:
        res += r[0].astype(F32)
    o_ref[0] = res.astype(BF)


def layer_step(cols, att, w, width, recvs):
    tokens, half = att[0].shape
    steps = cols.shape[0]
    sub = 2
    n = width // sub
    return pl.pallas_call(
        layer_kernel,
        grid_spec=pltpu.PrefetchScalarGridSpec(
            num_scalar_prefetch=1,
            grid=(steps, sub),
            in_specs=[
                pl.BlockSpec((tokens, half), lambda j, s, *_: (0, 0)),
                pl.BlockSpec((tokens, half), lambda j, s, *_: (0, 0)),
                pl.BlockSpec((w.shape[0], n), lambda j, s, c: (0, c[j] * sub + s)),
                *[pl.BlockSpec((1, tokens, n), lambda j, s, *_, at=at: (at, 0, s)) for _, at in recvs],
            ],
            out_specs=pl.BlockSpec((1, tokens, n), lambda j, s, *_: (j, 0, s)),
        ),
        out_shape=jax.ShapeDtypeStruct((steps, tokens, width), BF),
        compiler_params=params(BIG),
        name="layer_step",
    )(cols, att[0], att[1], w, *[r for r, _ in recvs])


def swap(x, axis, bits):
    n = lax.axis_size(axis)
    return lax.ppermute(x, axis, [(i, i ^ bits) for i in range(n)])


def after(x, *deps):
    return lax.optimization_barrier((x, *deps))[0]


def shards(queries, token_keys, token_values, out_weight, out_grad):
    pos = lax.axis_index("seq").astype(jnp.int32)
    tp = lax.axis_index("tp").astype(jnp.int32)
    seq_count, tp_count = lax.axis_size("seq"), lax.axis_size("tp")
    tokens, feats = queries.shape
    width = out_weight.shape[1]
    pos1 = pos[None]
    right_perm = [(i, i + 1) for i in range(seq_count - 1)]
    left_perm = [(i + 1, i) for i in range(seq_count - 1)]

    near, far_own, from_left, from_right = [], [], [], []
    for half in range(HALVES):
        n, f, to_left, to_right = pool(token_keys, token_values, half)
        near.append(n)
        far_own.append(f)
        from_left.append(lax.ppermute(to_right, "seq", right_perm))
        from_right.append(lax.ppermute(to_left, "seq", left_perm))
    far_all = jnp.concatenate(far_own, axis=2)
    far_all = jnp.broadcast_to(far_all, (seq_count, *far_all.shape))
    far_all = lax.all_to_all(far_all, "seq", 0, 0, tiled=True)
    far = jnp.moveaxis(far_all, 0, 1).reshape(2, -1, feats)
    attn_grad = dot(out_grad, out_weight, 1, 1).astype(BF)
    bias = level_bias(pos, tokens // FB, near[0].shape[1], far.shape[1], tokens, seq_count)

    att, attt, lse = zip(
        *[
            forward(seq_count, pos1, queries, token_keys, token_values, from_left[h], from_right[h], near[h], far, bias, h)
            for h in range(HALVES)
        ]
    )

    part = width // seq_count
    cols = block_order(pos)
    recv1 = [None] * UNITS
    for h in range(HALVES):
        units = list(range(h * UNITS // HALVES, (h + 1) * UNITS // HALVES))
        out = weight_step(cols, attt, out_grad, part, units, 8, 8, [], False)
        for u, x in zip(units, out):
            recv1[u] = (swap(x, "seq", ROUTE[u][1] << SHIFT[ROUTE[u][0]]), False)

    c, zl = tp & 1, tp >> 1
    lwidth = width // tp_count
    lcols = jnp.stack([zl, zl ^ 1]) * 2
    lgot1 = swap(layer_step(lcols + (c ^ 1), att, out_weight, lwidth, []), "tp", 1)

    dq, gk, gv, sl, sr, gfar = backward(
        seq_count, pos1, queries, token_keys, token_values, from_left, from_right, near, far, bias, attn_grad, att, lse
    )
    back_left = lax.ppermute(sr, "seq", right_perm)
    back_right = lax.ppermute(sl, "seq", left_perm)

    lgot2 = swap(layer_step(lcols[1:] + c, att, out_weight, lwidth, [(lgot1, 1)]), "tp", 2)

    every = list(range(UNITS))
    out = weight_step(cols, attt, out_grad, part, every, 4, 4, [recv1], False)
    recv2 = [(swap(x, "seq", ROUTE[u][2] << SHIFT[ROUTE[u][0]]), False) for u, x in enumerate(out)]
    far_parts = jnp.moveaxis(gfar.reshape(2, seq_count, -1, feats), 1, 0)
    far_sum = lax.all_to_all(far_parts, "seq", 0, 0, tiled=True).astype(F32).sum(axis=0)
    layer_out = layer_step(lcols[:1] + c, att, out_weight, lwidth, [(lgot1, 0), (lgot2, 0)])[0]

    got = [recv1, recv2]
    for step, (start, count) in enumerate(((2, 2), (1, 1))):
        out = weight_step(cols, attt, out_grad, part, every, start, count, got, True)
        moved = [swap(x, "seq", SECOND[p][step] << SHIFT[1 - ROUTE[2 * p][0]]) for p, x in enumerate(out)]
        got.append([(moved[u // 2], True) for u in every])
    zh = pos & 1
    zgot = swap(weight_last(cols, attt, out_grad, part, zh ^ 1, got, None, 1.0, BF), "seq", 1)
    weight_grad = weight_last(cols, attt, out_grad, part, zh, got, zgot, 1.0 / math.sqrt(tokens * seq_count), F32)

    key_grad, value_grad = combine(gk, gv, back_left, back_right, far_sum)
    return layer_out, dq, key_grad, value_grad, weight_grad


def solution(mesh):
    return jax.shard_map(
        shards,
        mesh=mesh,
        in_specs=(P("seq", "tp"), P("seq", "tp"), P("seq", "tp"), P("tp", None), P("seq", None)),
        out_specs=(P("seq", "tp"), P("seq", "tp"), P("seq", "tp"), P("seq", "tp"), P("tp", "seq")),
        check_vma=False,
    )
```

```python
import functools
import math

import jax
import jax.numpy as jnp
from jax import lax
from jax.experimental import pallas as pl
from jax.experimental.pallas import tpu as pltpu
from jax.sharding import PartitionSpec as P

DH = 128
FB = 128
P1 = 16
P2 = 256
BF = jnp.bfloat16
F32 = jnp.float32
NEG = -1e30
LOG2E = math.log2(math.e)
MB = 1024 * 1024
HALVES = 2
BIG = 20
SMALL = pl.CostEstimate(flops=1000, bytes_accessed=1000, transcendentals=0)


def dot(a, b, ca, cb):
    return lax.dot_general(a, b, (((ca,), (cb,)), ((), ())), preferred_element_type=F32)


def pinned(*args):
    return [pltpu.with_memory_space_constraint(a, pltpu.HBM) for a in args]


def params(limit):
    return pltpu.CompilerParams(vmem_limit_bytes=limit * MB)


def pool_kernel(k_ref, v_ref, near_ref, far_ref, left_ref, right_ref):
    rows = k_ref.shape[0]
    for i, ref in enumerate((k_ref, v_ref)):
        x = ref[...].astype(F32)
        s16 = x.reshape(rows // P1, P1, x.shape[1]).sum(axis=1)
        near = (s16 * (1.0 / P1)).astype(BF)
        far = s16.reshape(rows // P2, P2 // P1, x.shape[1]).sum(axis=1) * (1.0 / P2)
        near_ref[i] = near
        far_ref[i] = far.astype(BF)
        left_ref[i, :FB] = ref[:FB]
        right_ref[i, :FB] = ref[rows - FB :]
        left_ref[i, FB:] = near
        right_ref[i, FB:] = near


def pool(k, v, half):
    rows, feats = k.shape[0], k.shape[1] // HALVES
    nr, fr = rows // P1, rows // P2
    cols = 256
    per = feats // cols
    blk = lambda r: pl.BlockSpec((2, r, cols), lambda j: (0, 0, j))
    out = lambda r: pltpu.HBM((2, r, feats), BF)
    return pl.pallas_call(
        pool_kernel,
        grid=(per,),
        in_specs=[pl.BlockSpec((rows, cols), lambda j: (0, half * per + j))] * 2,
        out_specs=[blk(nr), blk(fr), blk(FB + nr), blk(FB + nr)],
        out_shape=[out(nr), out(fr), out(FB + nr), out(FB + nr)],
        compiler_params=params(BIG),
        cost_estimate=SMALL,
        name="pool",
    )(*pinned(k, v))


def level_bias(position, blocks, pooled_rows, coarse_count, tokens_here, seq_count):
    group_ids = jnp.arange(3 * pooled_rows, dtype=jnp.int32)
    group_dev = group_ids // pooled_rows
    absent = ((group_dev == 0) & (position == 0)) | ((group_dev == 2) & (position == seq_count - 1))
    block_ids = jnp.arange(blocks, dtype=jnp.int32)[:, None]
    distance = group_ids[None, :] * P1 // FB - blocks - block_ids
    near = jnp.where(absent[None, :] | (jnp.abs(distance) <= 1), NEG, math.log(P1) * LOG2E)
    coarse_dev = jnp.arange(coarse_count, dtype=jnp.int32) * P2 // tokens_here
    far = jnp.where(jnp.abs(coarse_dev - position) > 1, math.log(P2) * LOG2E, NEG)
    far = jnp.broadcast_to(far[None, :], (blocks, coarse_count))
    bias = jnp.concatenate([near, far], axis=1).astype(F32)
    return jnp.broadcast_to(bias[:, :, None], (*bias.shape, FB))


def gathered(i, left_ref, own_ref, right_ref, near_ref, far_ref):
    keys = jnp.concatenate([left_ref[i, :FB], own_ref[...], right_ref[i, :FB]], axis=0)
    coarse = jnp.concatenate([left_ref[i, FB:], near_ref[i], right_ref[i, FB:], far_ref[i]], axis=0)
    return keys, coarse


def scores(b, blocks, pos_ref, seq_count, q, keys, coarse_scores, bias_ref):
    scale = LOG2E / math.sqrt(DH)
    qb = q[b * FB : (b + 1) * FB]
    fine = dot(keys[b * FB : (b + 3) * FB], qb, 1, 1) * scale
    if b == 0:
        edge = jnp.where(pos_ref[0] == 0, NEG, 0.0).astype(F32)
        fine = jnp.concatenate([fine[:FB] + edge, fine[FB:]], axis=0)
    if b == blocks - 1:
        edge = jnp.where(pos_ref[0] == seq_count - 1, NEG, 0.0).astype(F32)
        fine = jnp.concatenate([fine[: 2 * FB], fine[2 * FB :] + edge], axis=0)
    coarse = coarse_scores[:, b * FB : (b + 1) * FB] * scale + bias_ref[b]
    return fine, coarse


def fwd_kernel(seq_count, pos_ref, q_ref, k_ref, v_ref, left_ref, right_ref, near_ref, far_ref, bias_ref, att_ref, attt_ref, lse_ref):
    blocks = q_ref.shape[0] // FB
    q = q_ref[...]
    keys, ckeys = gathered(0, left_ref, k_ref, right_ref, near_ref, far_ref)
    vals, cvals = gathered(1, left_ref, v_ref, right_ref, near_ref, far_ref)
    vals_t, cvals_t = vals.T, cvals.T
    csc = dot(ckeys, q, 1, 1)
    raw = [scores(b, blocks, pos_ref, seq_count, q, keys, csc, bias_ref) for b in range(blocks)]
    peaks = [jnp.maximum(fine.max(axis=0, keepdims=True), coarse.max(axis=0, keepdims=True)) for fine, coarse in raw]
    for b, ((fine, coarse), peak) in enumerate(zip(raw, peaks)):
        pf = jnp.exp2(fine - peak)
        pc = jnp.exp2(coarse - peak)
        total = pf.sum(axis=0, keepdims=True) + pc.sum(axis=0, keepdims=True)
        lse_ref[0, :, b * FB : (b + 1) * FB] = peak + jnp.log2(total)
        out_t = dot(vals_t[:, b * FB : (b + 3) * FB], pf.astype(BF), 1, 0) + dot(cvals_t, pc.astype(BF), 1, 0)
        out_t = (out_t * (1.0 / total)).astype(BF)
        attt_ref[:, b * FB : (b + 1) * FB] = out_t
        att_ref[b * FB : (b + 1) * FB, :] = out_t.T


def bwd_kernel(
    seq_count, pos_ref, q_ref, k_ref, v_ref, left_ref, right_ref, near_ref, far_ref, bias_ref, do_ref, att_ref, lse_ref,
    dq_ref, gk_ref, gv_ref, sl_ref, sr_ref, gfar_ref, p_ref, ds_ref, cp_ref, cds_ref,
):
    blocks = q_ref.shape[0] // FB
    own = blocks * FB
    inv = 1.0 / math.sqrt(DH)
    q, do = q_ref[...], do_ref[...]
    keys, ckeys = gathered(0, left_ref, k_ref, right_ref, near_ref, far_ref)
    vals, cvals = gathered(1, left_ref, v_ref, right_ref, near_ref, far_ref)
    keys_t, ckeys_t = keys.T, ckeys.T
    csc = dot(ckeys, q, 1, 1)
    cdp = dot(cvals, do, 1, 1)
    delta_all = (do.astype(F32) * att_ref[...].astype(F32)).T.sum(axis=0, keepdims=True)
    for b in range(blocks):
        cols = slice(b * FB, (b + 1) * FB)
        fine, coarse = scores(b, blocks, pos_ref, seq_count, q, keys, csc, bias_ref)
        lse = lse_ref[0, :, cols]
        delta = delta_all[:, cols]
        pf = jnp.exp2(fine - lse)
        pc = jnp.exp2(coarse - lse)
        dpf = dot(vals[b * FB : (b + 3) * FB], do[cols], 1, 1)
        dsf = (pf * (dpf - delta)).astype(BF)
        dsc = (pc * (cdp[:, cols] - delta)).astype(BF)
        p_ref[b * FB : (b + 3) * FB, cols] = pf.astype(BF)
        ds_ref[b * FB : (b + 3) * FB, cols] = dsf
        cp_ref[:, cols] = pc.astype(BF)
        cds_ref[:, cols] = dsc
        dq_t = dot(keys_t[:, b * FB : (b + 3) * FB], dsf, 1, 0) + dot(ckeys_t, dsc, 1, 0)
        dq_ref[cols, :] = (dq_t * inv).astype(BF).T
    nr = near_ref.shape[1]
    for i, (src, csrc, rhs, mul, g_ref) in enumerate(((ds_ref, cds_ref, q, inv, gk_ref), (p_ref, cp_ref, do, 1.0, gv_ref))):
        cg = dot(csrc[...], rhs, 1, 0) * mul
        sl_ref[i, FB:] = cg[:nr].astype(BF)
        sr_ref[i, FB:] = cg[2 * nr : 3 * nr].astype(BF)
        gfar_ref[i] = cg[3 * nr :].astype(BF)
        mine = cg[nr : 2 * nr] * (1.0 / P1)
        for c in range(blocks + 2):
            lo, hi = max(0, c - 2), min(blocks, c + 1)
            part = dot(src[c * FB : (c + 1) * FB, lo * FB : hi * FB], rhs[lo * FB : hi * FB], 1, 0) * mul
            if c == 0:
                sl_ref[i, :FB] = part.astype(BF)
            elif c == blocks + 1:
                sr_ref[i, :FB] = part.astype(BF)
            else:
                r = c - 1
                per = FB // P1
                spread = jnp.broadcast_to(mine[r * per : (r + 1) * per, None, :], (per, P1, DH)).reshape(FB, DH)
                g_ref[r * FB : (r + 1) * FB, :] = part + spread


def forward(seq_count, pos, q, k, v, left, right, near, far, bias, half):
    tokens, feats = q.shape[0], q.shape[1] // HALVES
    heads, blocks = feats // DH, tokens // FB
    tok = pl.BlockSpec((tokens, DH), lambda h, *_: (0, half * heads + h))
    lev = lambda a: pl.BlockSpec((2, a.shape[1], DH), lambda h, *_: (0, 0, h))
    far_spec = pl.BlockSpec((2, far.shape[1], DH), lambda h, *_: (0, 0, half * heads + h))
    bias_spec = pl.BlockSpec(bias.shape, lambda h, *_: (0, 0, 0))
    return pl.pallas_call(
        functools.partial(fwd_kernel, seq_count),
        grid_spec=pltpu.PrefetchScalarGridSpec(
            num_scalar_prefetch=1,
            grid=(heads,),
            in_specs=[tok, tok, tok, lev(left), lev(right), lev(near), far_spec, bias_spec],
            out_specs=[
                pl.BlockSpec((tokens, DH), lambda h, *_: (0, h)),
                pl.BlockSpec((DH, tokens), lambda h, *_: (h, 0)),
                pl.BlockSpec((1, 1, tokens), lambda h, *_: (h, 0, 0)),
            ],
        ),
        out_shape=[
            jax.ShapeDtypeStruct((tokens, feats), BF),
            jax.ShapeDtypeStruct((feats, tokens), BF),
            jax.ShapeDtypeStruct((heads, 1, tokens), F32),
        ],
        compiler_params=params(BIG),
        cost_estimate=SMALL,
        name="attend",
    )(pos, *pinned(q, k, v, left, right, near, far, bias))


def bwd_halves_kernel(seq_count, pos_ref, q_ref, k_ref, v_ref, *refs):
    per = pl.num_programs(0) // HALVES
    first = pl.program_id(0) < per
    pairs, rest = refs[: 5 * HALVES], refs[5 * HALVES :]
    picked = [jnp.where(first, pairs[2 * i][...], pairs[2 * i + 1][...]) for i in range(5)]
    left, right, near, att, lse = picked
    far_ref, bias_ref, do_ref, *outs = rest
    bwd_kernel(seq_count, pos_ref, q_ref, k_ref, v_ref, left, right, near, far_ref, bias_ref, do_ref, att, lse, *outs)


def backward(seq_count, pos, q, k, v, left, right, near, far, bias, do, att, lse):
    tokens, feats = q.shape
    heads = feats // DH
    per = heads // HALVES
    halo, nr, fr = left[0].shape[1], near[0].shape[1], far.shape[1]
    coarse = 3 * nr + fr
    tok = pl.BlockSpec((tokens, DH), lambda h, *_: (0, h))
    lev = lambda r: pl.BlockSpec((2, r, DH), lambda h, *_: (0, 0, h))
    at = (lambda h: jnp.minimum(h, per - 1), lambda h: jnp.maximum(h - per, 0))
    pairs, pair_specs = [], []
    for x in (left, right, near, att, lse):
        for half, pick in enumerate(at):
            pairs.append(x[half])
            if x is att:
                pair_specs.append(pl.BlockSpec((tokens, DH), lambda h, *_, p=pick: (0, p(h))))
            elif x is lse:
                pair_specs.append(pl.BlockSpec((1, 1, tokens), lambda h, *_, p=pick: (p(h), 0, 0)))
            else:
                pair_specs.append(pl.BlockSpec((2, x[half].shape[1], DH), lambda h, *_, p=pick: (0, 0, p(h))))
    return pl.pallas_call(
        functools.partial(bwd_halves_kernel, seq_count),
        grid_spec=pltpu.PrefetchScalarGridSpec(
            num_scalar_prefetch=1,
            grid=(heads,),
            in_specs=[tok, tok, tok, *pair_specs, lev(fr), pl.BlockSpec(bias.shape, lambda h, *_: (0, 0, 0)), tok],
            out_specs=[tok, tok, tok, lev(halo), lev(halo), lev(fr)],
            scratch_shapes=[
                pltpu.VMEM((tokens + 2 * FB, tokens), BF),
                pltpu.VMEM((tokens + 2 * FB, tokens), BF),
                pltpu.VMEM((coarse, tokens), BF),
                pltpu.VMEM((coarse, tokens), BF),
            ],
        ),
        out_shape=[
            pltpu.HBM((tokens, feats), BF),
            pltpu.HBM((tokens, feats), F32),
            pltpu.HBM((tokens, feats), F32),
            jax.ShapeDtypeStruct((2, halo, feats), BF),
            jax.ShapeDtypeStruct((2, halo, feats), BF),
            jax.ShapeDtypeStruct((2, fr, feats), BF),
        ],
        compiler_params=params(BIG),
        cost_estimate=SMALL,
        name="attend_grad",
    )(pos, *pinned(q, k, v, *pairs, far, bias), do)


def combine_kernel(gk_ref, gv_ref, left_ref, right_ref, far_ref, ok_ref, ov_ref):
    rows, width = gk_ref.shape
    for i, (g_ref, o_ref) in enumerate(((gk_ref, ok_ref), (gv_ref, ov_ref))):
        near = (left_ref[i, FB:].astype(F32) + right_ref[i, FB:].astype(F32)) * (1.0 / P1)
        per = FB // P1
        for r in range(rows // FB):
            part = g_ref[r * FB : (r + 1) * FB]
            part += jnp.broadcast_to(near[r * per : (r + 1) * per, None, :], (per, P1, width)).reshape(FB, width)
            g = r * FB // P2
            part += far_ref[i, g : g + 1] * (1.0 / P2)
            if r == 0:
                part += left_ref[i, :FB].astype(F32)
            if r == rows // FB - 1:
                part += right_ref[i, :FB].astype(F32)
            o_ref[r * FB : (r + 1) * FB] = part.astype(BF)


def combine(gk, gv, from_left, from_right, far):
    rows, feats = gk.shape
    cols = 256
    tok = pl.BlockSpec((rows, cols), lambda j: (0, j))
    lev = lambda r: pl.BlockSpec((2, r, cols), lambda j: (0, 0, j))
    halo = from_left.shape[1]
    return pl.pallas_call(
        combine_kernel,
        grid=(feats // cols,),
        in_specs=[tok, tok, lev(halo), lev(halo), lev(far.shape[1])],
        out_specs=[tok, tok],
        out_shape=[jax.ShapeDtypeStruct((rows, feats), BF)] * 2,
        compiler_params=params(BIG),
        cost_estimate=SMALL,
        name="combine",
    )(*pinned(gk, gv, from_left, from_right, far))


UNITS = 4
ROUTE = ((0, 1, 3), (0, 3, 1), (1, 1, 3), (1, 3, 1))
SECOND = ((1, 3), (3, 1))
SHIFT = (3, 1)


def block_order(pos):
    coord = ((pos >> 3) & 3, (pos >> 1) & 3)
    rows = []
    for u, (axis, k1, k2) in enumerate(ROUTE):
        m1, m2 = SECOND[u // 2]
        first = coord[axis] ^ jnp.array([0, k2, k1, k1 ^ k2], jnp.int32)
        second = coord[1 - axis] ^ jnp.array([0, m2, m1, m1 ^ m2], jnp.int32)
        at = first[:, None] * 4 + second[None, :] if axis == 0 else second[None, :] * 4 + first[:, None]
        rows.append(at.reshape(-1))
    return jnp.stack(rows).astype(jnp.int32)


def weight_kernel(n_units, per, n_recv, pair_out, cols_ref, *refs):
    atts, ogs = refs[:n_units], refs[n_units : n_units + n_units * per]
    recvs = refs[n_units + n_units * per : n_units + n_units * per + n_recv]
    outs = refs[n_units + n_units * per + n_recv :]
    for u in range(n_units):
        for b in range(per):
            res = dot(atts[u][...], ogs[u * per + b][...], 1, 0)
            rows, width = res.shape[0], res.shape[1] // 2
            for z in range(2):
                part = res[:, z * width : (z + 1) * width]
                for r in recvs[u::n_units]:
                    part += r[b, z].astype(F32)
                if pair_out:
                    outs[u // 2][b, z, (u % 2) * rows : (u % 2 + 1) * rows] = part.astype(BF)
                else:
                    outs[u][b, z] = part.astype(BF)


def weight_step(cols, attt, og, width, units, start, count, per, recvs, pair_out):
    tokens = attt[0].shape[1]
    rows = attt[0].shape[0] * HALVES // UNITS
    n = len(units)
    per_half = UNITS // HALVES
    in_specs, args = [], []
    for u in units:
        in_specs.append(pl.BlockSpec((rows, tokens), lambda j, *_, u=u: (u % per_half, 0)))
        args += pinned(attt[u // per_half]) if recvs else [attt[u // per_half]]
    for u in units:
        for b in range(per):
            in_specs.append(pl.BlockSpec((tokens, 2 * width), lambda j, c, u=u, b=b: (0, c[u, start + j * per + b])))
            args += pinned(og)
    for i, step in enumerate(recvs):
        for u in units:
            r, paired = step[u]
            if i < len(recvs) - 1:
                (r,) = pinned(r)
            at = u % 2 if paired else 0
            in_specs.append(pl.BlockSpec((per, 2, rows, width), lambda j, *_, at=at: (start // per + j, 0, at, 0)))
            args.append(r)
    n_out = n // 2 if pair_out else n
    out_rows = 2 * rows if pair_out else rows
    return pl.pallas_call(
        functools.partial(weight_kernel, n, per, len(recvs) * n, pair_out),
        grid_spec=pltpu.PrefetchScalarGridSpec(
            num_scalar_prefetch=1,
            grid=(count // per,),
            in_specs=in_specs,
            out_specs=[pl.BlockSpec((per, 2, out_rows, width), lambda j, *_: (j, 0, 0, 0))] * n_out,
        ),
        out_shape=[jax.ShapeDtypeStruct((count, 2, out_rows, width), BF)] * n_out,
        compiler_params=params(BIG),
        cost_estimate=SMALL,
        name="weight_step",
    )(cols, *args)


def weight_last_kernel(n_recv, table_ref, *refs):
    send_ref, keep_ref = refs[-2:]
    atts, ogs = refs[:UNITS], refs[UNITS : 2 * UNITS]
    recvs = refs[2 * UNITS : 2 * UNITS + n_recv]
    own_first = table_ref[UNITS] == 0
    rows = atts[0].shape[0]
    for u in range(UNITS):
        res = dot(atts[u][...], ogs[u][...], 1, 0)
        width = res.shape[1] // 2
        parts = []
        for z in range(2):
            part = res[:, z * width : (z + 1) * width]
            for r in recvs[u::UNITS]:
                part += r[0, z].astype(F32)
            parts.append(part)
        at = slice(u * rows, (u + 1) * rows)
        keep_ref[at] = jnp.where(own_first, parts[0], parts[1])
        send_ref[at] = jnp.where(own_first, parts[1], parts[0]).astype(BF)


def weight_last(cols, attt, og, width, z, recvs):
    tokens = attt[0].shape[1]
    rows = attt[0].shape[0] * HALVES // UNITS
    per_half = UNITS // HALVES
    table = jnp.concatenate([cols[:, 0], z[None]])
    in_specs, args = [], []
    for u in range(UNITS):
        in_specs.append(pl.BlockSpec((rows, tokens), lambda j, *_, u=u: (u % per_half, 0)))
        args += pinned(attt[u // per_half])
    for u in range(UNITS):
        in_specs.append(pl.BlockSpec((tokens, 2 * width), lambda j, c, u=u: (0, c[u])))
        args += pinned(og)
    for i, step in enumerate(recvs):
        for u in range(UNITS):
            r, paired = step[u]
            if i < len(recvs) - 1:
                (r,) = pinned(r)
            at = u % 2 if paired else 0
            in_specs.append(pl.BlockSpec((1, 2, rows, width), lambda j, c, at=at: (0, 0, at, 0)))
            args.append(r)
    full = pl.BlockSpec((UNITS * rows, width), lambda j, *_: (0, 0))
    return pl.pallas_call(
        functools.partial(weight_last_kernel, len(recvs) * UNITS),
        grid_spec=pltpu.PrefetchScalarGridSpec(num_scalar_prefetch=1, grid=(1,), in_specs=in_specs, out_specs=[full, full]),
        out_shape=[jax.ShapeDtypeStruct((UNITS * rows, width), t) for t in (BF, F32)],
        compiler_params=params(BIG),
        cost_estimate=SMALL,
        name="weight_last",
    )(table, *args)


def project_kernel(og_ref, w_ref, o_ref):
    n = o_ref.shape[1]
    at = pl.multiple_of(pl.program_id(0) * n, n)
    o_ref[...] = dot(og_ref[...], w_ref[pl.ds(at, n), :], 1, 1).astype(BF)


def project(og, w):
    tokens, feats = og.shape[0], w.shape[0]
    n = 256
    return pl.pallas_call(
        project_kernel,
        grid=(feats // n,),
        in_specs=[pl.BlockSpec(memory_space=pltpu.VMEM)] * 2,
        out_specs=pl.BlockSpec((tokens, n), lambda j: (0, j)),
        out_shape=jax.ShapeDtypeStruct((tokens, feats), BF),
        compiler_params=params(BIG),
        cost_estimate=SMALL,
        name="project",
    )(og, w)


def project_kernel(cols_ref, a0_ref, a1_ref, og_ref, w_ref, send_ref, keep_ref, grad_ref, acc_ref):
    step = pl.program_id(0)
    half = a0_ref.shape[1]
    part = dot(og_ref[...], w_ref[...], 1, 1)

    @pl.when(step == 0)
    def _():
        acc_ref[...] = part

    @pl.when(step > 0)
    def _():
        acc_ref[...] += part

    res = (dot(a0_ref[...], w_ref[:half], 1, 0) + dot(a1_ref[...], w_ref[half:], 1, 0)).astype(BF)

    @pl.when(step < pl.num_programs(0) // 2)
    def _():
        send_ref[0] = res

    @pl.when(step >= pl.num_programs(0) // 2)
    def _():
        keep_ref[0] = res

    @pl.when(step == pl.num_programs(0) - 1)
    def _():
        grad_ref[...] = acc_ref[...].astype(BF)


def project(cols, att, og, w, width):
    tokens, half = att[0].shape
    feats = w.shape[0]
    sub = 1
    n = width // sub
    parts = cols.shape[0]
    steps = parts * sub
    mid = steps // 2
    whole = lambda r, c: pl.BlockSpec((r, c), lambda s, *_: (0, 0))
    first = lambda s: jnp.minimum(s, mid - 1)
    later = lambda s: jnp.maximum(s - mid, 0)
    return pl.pallas_call(
        project_kernel,
        grid_spec=pltpu.PrefetchScalarGridSpec(
            num_scalar_prefetch=1,
            grid=(steps,),
            in_specs=[
                whole(tokens, half),
                whole(tokens, half),
                pl.BlockSpec((tokens, n), lambda s, c: (0, c[s // sub] * sub + s % sub)),
                pl.BlockSpec((feats, n), lambda s, c: (0, c[s // sub] * sub + s % sub)),
            ],
            out_specs=[
                pl.BlockSpec((1, tokens, n), lambda s, *_: (first(s) // sub, 0, first(s) % sub)),
                pl.BlockSpec((1, tokens, n), lambda s, *_: (later(s) // sub, 0, later(s) % sub)),
                whole(tokens, feats),
            ],
            scratch_shapes=[pltpu.VMEM((tokens, feats), F32)],
        ),
        out_shape=[
            jax.ShapeDtypeStruct((parts // 2, tokens, width), BF),
            pltpu.HBM((parts // 2, tokens, width), BF),
            jax.ShapeDtypeStruct((tokens, feats), BF),
        ],
        compiler_params=params(BIG),
        cost_estimate=SMALL,
        name="project",
    )(cols, *att, *pinned(og, w))


def swap(x, axis, bits):
    n = lax.axis_size(axis)
    return lax.ppermute(x, axis, [(i, i ^ bits) for i in range(n)])


def after(x, *deps):
    return lax.optimization_barrier((x, *deps))[0]


def own_rows(x, pos, seq_count):
    bit = seq_count // 2
    while bit:
        low = (pos & bit) == 0
        half = x.shape[1] // 2
        a, b = x[:, :half], x[:, half:]
        got = swap(jnp.where(low, b, a), "seq", bit)
        x = jnp.where(low, a, b).astype(F32) + got.astype(F32)
        bit //= 2
        if bit:
            x = x.astype(BF)
    return x


def shards(queries, token_keys, token_values, out_weight, out_grad):
    pos = lax.axis_index("seq").astype(jnp.int32)
    tp = lax.axis_index("tp").astype(jnp.int32)
    seq_count, tp_count = lax.axis_size("seq"), lax.axis_size("tp")
    tokens, feats = queries.shape
    width = out_weight.shape[1]
    pos1 = pos[None]
    right_perm = [(i, i + 1) for i in range(seq_count - 1)]
    left_perm = [(i + 1, i) for i in range(seq_count - 1)]

    pools = [pool(token_keys, token_values, half) for half in range(HALVES)]
    near = [p[0] for p in pools]
    far_own = jnp.concatenate([p[1] for p in pools], axis=2)
    from_left, from_right = [], []
    for half, (_, _, to_left, to_right) in enumerate(pools):
        if half > 0:
            to_left, to_right = lax.optimization_barrier((to_left, to_right, from_left[0], from_right[0]))[:2]
        from_left.append(lax.ppermute(to_right, "seq", right_perm))
        from_right.append(lax.ppermute(to_left, "seq", left_perm))
    far_all = jnp.broadcast_to(far_own, (seq_count, *far_own.shape))
    far_all = lax.all_to_all(far_all, "seq", 0, 0, tiled=True)
    far = jnp.moveaxis(far_all, 0, 1).reshape(2, -1, feats)
    bias = level_bias(pos, tokens // FB, near[0].shape[1], far.shape[1], tokens, seq_count)

    part = width // seq_count
    cols = block_order(pos)
    recv1, recv2 = [None] * UNITS, [None] * UNITS
    att, attt, lse = [], [], []
    half_units = [list(range(h * UNITS // HALVES, (h + 1) * UNITS // HALVES)) for h in range(HALVES)]
    out = None
    for h, units in enumerate(half_units):
        q = queries if out is None else after(queries, *out)
        a, at, ls = forward(seq_count, pos1, q, token_keys, token_values, from_left[h], from_right[h], near[h], far, bias, h)
        att.append(a)
        attt.append(at)
        lse.append(ls)
        table = after(cols, from_left[1], from_right[1]) if h == 0 else cols
        out = weight_step(table, attt, out_grad, part, units, 8, 8, 4, [], False)
        for u, x in zip(units, out):
            recv1[u] = (swap(x, "seq", ROUTE[u][1] << SHIFT[ROUTE[u][0]]), False)

    def second(pair, dep):
        out = weight_step(after(cols, *dep), attt, out_grad, part, half_units[pair], 4, 4, 2, [recv1], False)
        for u, x in zip(half_units[pair], out):
            recv2[u] = (swap(x, "seq", ROUTE[u][2] << SHIFT[ROUTE[u][0]]), False)
        return out

    recv3, recv4 = [None] * UNITS, [None] * UNITS

    def along_other(pair, step, dep):
        got = [recv1, recv2, recv3][: 2 + step]
        start = 2 - step
        out = weight_step(after(cols, *dep), attt, out_grad, part, half_units[pair], start, start, start, got, True)
        moved = swap(out[0], "seq", SECOND[pair][step] << SHIFT[1 - ROUTE[2 * pair][0]])
        for u in half_units[pair]:
            (recv3, recv4)[step][u] = (moved, True)
        return out

    c, zl = tp & 1, tp >> 1
    lwidth = width // tp_count
    lcols = jnp.stack([zl, zl ^ 1]) * 2
    lorder = jnp.concatenate([lcols + (c ^ 1), lcols + c])
    lsend1, lkeep, attn_grad = project(lorder, (after(att[0], *out), att[1]), out_grad, out_weight, lwidth)
    lgot1 = swap(lsend1, "tp", 1)

    out = second(0, [attn_grad])
    dq, gk, gv, sl, sr, gfar = backward(
        seq_count, pos1, after(queries, *out), token_keys, token_values, from_left, from_right, near, far, bias, attn_grad, att, lse
    )
    back_left = lax.ppermute(sr, "seq", right_perm)
    back_right = lax.ppermute(sl, "seq", left_perm)
    out = along_other(0, 0, [gfar])
    out = second(1, out)
    lsend2 = (lkeep[1].astype(F32) + lgot1[1].astype(F32)).astype(BF)
    lgot2 = swap(lsend2, "tp", 2)
    out = along_other(0, 1, out)
    far_sum = own_rows(after(gfar, *out), pos, seq_count)
    out = along_other(1, 0, out)
    out = along_other(1, 1, [*out, back_left, back_right])
    got = [recv1, recv2, recv3, recv4]
    zsend, zkeep = weight_last(cols, attt, out_grad, part, pos & 1, got)
    zgot = swap(zsend, "seq", 1)
    layer_out = (lkeep[0].astype(F32) + lgot1[0].astype(F32) + lgot2.astype(F32)).astype(BF)
    key_grad, value_grad = combine(gk, gv, back_left, back_right, far_sum)
    weight_grad = (zkeep + zgot.astype(F32)) * (1.0 / math.sqrt(tokens * seq_count))
    return layer_out, dq, key_grad, value_grad, weight_grad


def solution(mesh):
    return jax.shard_map(
        shards,
        mesh=mesh,
        in_specs=(P("seq", "tp"), P("seq", "tp"), P("seq", "tp"), P("tp", None), P("seq", None)),
        out_specs=(P("seq", "tp"), P("seq", "tp"), P("seq", "tp"), P("seq", "tp"), P("tp", "seq")),
        check_vma=False,
    )
```

```python
import functools
import math

import jax
import jax.numpy as jnp
from jax import lax
from jax.experimental import pallas as pl
from jax.experimental.pallas import tpu as pltpu
from jax.sharding import PartitionSpec as P

DH = 128
FB = 128
P1 = 16
P2 = 256
BF = jnp.bfloat16
F32 = jnp.float32
NEG = -1e30
LOG2E = math.log2(math.e)
MB = 1024 * 1024
HALVES = 1
BIG = 20
SMALL = pl.CostEstimate(flops=1000, bytes_accessed=1000, transcendentals=0)


def dot(a, b, ca, cb):
    return lax.dot_general(a, b, (((ca,), (cb,)), ((), ())), preferred_element_type=F32)


def pinned(*args):
    return [pltpu.with_memory_space_constraint(a, pltpu.HBM) for a in args]


def params(limit):
    return pltpu.CompilerParams(vmem_limit_bytes=limit * MB)


def pool_kernel(k_ref, v_ref, near_ref, far_ref, left_ref, right_ref):
    rows = k_ref.shape[0]
    for i, ref in enumerate((k_ref, v_ref)):
        x = ref[...].astype(F32)
        s16 = x.reshape(rows // P1, P1, x.shape[1]).sum(axis=1)
        near = (s16 * (1.0 / P1)).astype(BF)
        far = s16.reshape(rows // P2, P2 // P1, x.shape[1]).sum(axis=1) * (1.0 / P2)
        near_ref[i] = near
        far_ref[i] = far.astype(BF)
        left_ref[i, :FB] = ref[:FB]
        right_ref[i, :FB] = ref[rows - FB :]
        left_ref[i, FB:] = near
        right_ref[i, FB:] = near


def pool(k, v, half):
    rows, feats = k.shape[0], k.shape[1] // HALVES
    nr, fr = rows // P1, rows // P2
    cols = 256
    per = feats // cols
    blk = lambda r: pl.BlockSpec((2, r, cols), lambda j: (0, 0, j))
    out = lambda r: pltpu.HBM((2, r, feats), BF)
    return pl.pallas_call(
        pool_kernel,
        grid=(per,),
        in_specs=[pl.BlockSpec((rows, cols), lambda j: (0, half * per + j))] * 2,
        out_specs=[blk(nr), blk(fr), blk(FB + nr), blk(FB + nr)],
        out_shape=[out(nr), out(fr), out(FB + nr), out(FB + nr)],
        compiler_params=params(BIG),
        cost_estimate=SMALL,
        name="pool",
    )(*pinned(k, v))


def level_bias(position, blocks, pooled_rows, coarse_count, tokens_here, seq_count):
    group_ids = jnp.arange(3 * pooled_rows, dtype=jnp.int32)
    group_dev = group_ids // pooled_rows
    absent = ((group_dev == 0) & (position == 0)) | ((group_dev == 2) & (position == seq_count - 1))
    block_ids = jnp.arange(blocks, dtype=jnp.int32)[:, None]
    distance = group_ids[None, :] * P1 // FB - blocks - block_ids
    near = jnp.where(absent[None, :] | (jnp.abs(distance) <= 1), NEG, math.log(P1) * LOG2E)
    coarse_dev = jnp.arange(coarse_count, dtype=jnp.int32) * P2 // tokens_here
    far = jnp.where(jnp.abs(coarse_dev - position) > 1, math.log(P2) * LOG2E, NEG)
    far = jnp.broadcast_to(far[None, :], (blocks, coarse_count))
    bias = jnp.concatenate([near, far], axis=1).astype(F32)
    return jnp.broadcast_to(bias[:, :, None], (*bias.shape, FB))


def gathered(i, left_ref, own_ref, right_ref, near_ref, far_ref):
    keys = jnp.concatenate([left_ref[i, :FB], own_ref[...], right_ref[i, :FB]], axis=0)
    coarse = jnp.concatenate([left_ref[i, FB:], near_ref[i], right_ref[i, FB:], far_ref[i]], axis=0)
    return keys, coarse


def scores(b, blocks, pos_ref, seq_count, q, keys, coarse_scores, bias_ref):
    scale = LOG2E / math.sqrt(DH)
    qb = q[b * FB : (b + 1) * FB]
    fine = dot(keys[b * FB : (b + 3) * FB], qb, 1, 1) * scale
    if b == 0:
        edge = jnp.where(pos_ref[0] == 0, NEG, 0.0).astype(F32)
        fine = jnp.concatenate([fine[:FB] + edge, fine[FB:]], axis=0)
    if b == blocks - 1:
        edge = jnp.where(pos_ref[0] == seq_count - 1, NEG, 0.0).astype(F32)
        fine = jnp.concatenate([fine[: 2 * FB], fine[2 * FB :] + edge], axis=0)
    coarse = coarse_scores[:, b * FB : (b + 1) * FB] * scale + bias_ref[b]
    return fine, coarse


def fwd_kernel(seq_count, pos_ref, q_ref, k_ref, v_ref, left_ref, right_ref, near_ref, far_ref, bias_ref, att_ref, attt_ref, lse_ref):
    blocks = q_ref.shape[0] // FB
    q = q_ref[...]
    keys, ckeys = gathered(0, left_ref, k_ref, right_ref, near_ref, far_ref)
    vals, cvals = gathered(1, left_ref, v_ref, right_ref, near_ref, far_ref)
    vals_t, cvals_t = vals.T, cvals.T
    csc = dot(ckeys, q, 1, 1)
    raw = [scores(b, blocks, pos_ref, seq_count, q, keys, csc, bias_ref) for b in range(blocks)]
    peaks = [jnp.maximum(fine.max(axis=0, keepdims=True), coarse.max(axis=0, keepdims=True)) for fine, coarse in raw]
    for b, ((fine, coarse), peak) in enumerate(zip(raw, peaks)):
        pf = jnp.exp2(fine - peak)
        pc = jnp.exp2(coarse - peak)
        total = pf.sum(axis=0, keepdims=True) + pc.sum(axis=0, keepdims=True)
        lse_ref[0, :, b * FB : (b + 1) * FB] = peak + jnp.log2(total)
        out_t = dot(vals_t[:, b * FB : (b + 3) * FB], pf.astype(BF), 1, 0) + dot(cvals_t, pc.astype(BF), 1, 0)
        out_t = (out_t * (1.0 / total)).astype(BF)
        attt_ref[:, b * FB : (b + 1) * FB] = out_t
        att_ref[b * FB : (b + 1) * FB, :] = out_t.T


def bwd_kernel(
    seq_count, pos_ref, q_ref, k_ref, v_ref, left_ref, right_ref, near_ref, far_ref, bias_ref, do_ref, att_ref, lse_ref,
    dq_ref, gk_ref, gv_ref, sl_ref, sr_ref, gfar_ref, p_ref, ds_ref, cp_ref, cds_ref,
):
    blocks = q_ref.shape[0] // FB
    own = blocks * FB
    inv = 1.0 / math.sqrt(DH)
    q, do = q_ref[...], do_ref[...]
    keys, ckeys = gathered(0, left_ref, k_ref, right_ref, near_ref, far_ref)
    vals, cvals = gathered(1, left_ref, v_ref, right_ref, near_ref, far_ref)
    keys_t, ckeys_t = keys.T, ckeys.T
    csc = dot(ckeys, q, 1, 1)
    cdp = dot(cvals, do, 1, 1)
    delta_all = (do.astype(F32) * att_ref[...].astype(F32)).T.sum(axis=0, keepdims=True)
    for b in range(blocks):
        cols = slice(b * FB, (b + 1) * FB)
        fine, coarse = scores(b, blocks, pos_ref, seq_count, q, keys, csc, bias_ref)
        lse = lse_ref[0, :, cols]
        delta = delta_all[:, cols]
        pf = jnp.exp2(fine - lse)
        pc = jnp.exp2(coarse - lse)
        dpf = dot(vals[b * FB : (b + 3) * FB], do[cols], 1, 1)
        dsf = (pf * (dpf - delta)).astype(BF)
        dsc = (pc * (cdp[:, cols] - delta)).astype(BF)
        p_ref[b * FB : (b + 3) * FB, cols] = pf.astype(BF)
        ds_ref[b * FB : (b + 3) * FB, cols] = dsf
        cp_ref[:, cols] = pc.astype(BF)
        cds_ref[:, cols] = dsc
        dq_t = dot(keys_t[:, b * FB : (b + 3) * FB], dsf, 1, 0) + dot(ckeys_t, dsc, 1, 0)
        dq_ref[cols, :] = (dq_t * inv).astype(BF).T
    nr = near_ref.shape[1]
    for i, (src, csrc, rhs, mul, g_ref) in enumerate(((ds_ref, cds_ref, q, inv, gk_ref), (p_ref, cp_ref, do, 1.0, gv_ref))):
        cg = dot(csrc[...], rhs, 1, 0) * mul
        sl_ref[i, FB:] = cg[:nr].astype(BF)
        sr_ref[i, FB:] = cg[2 * nr : 3 * nr].astype(BF)
        gfar_ref[i] = cg[3 * nr :].astype(BF)
        mine = cg[nr : 2 * nr] * (1.0 / P1)
        for c in range(blocks + 2):
            lo, hi = max(0, c - 2), min(blocks, c + 1)
            part = dot(src[c * FB : (c + 1) * FB, lo * FB : hi * FB], rhs[lo * FB : hi * FB], 1, 0) * mul
            if c == 0:
                sl_ref[i, :FB] = part.astype(BF)
            elif c == blocks + 1:
                sr_ref[i, :FB] = part.astype(BF)
            else:
                r = c - 1
                per = FB // P1
                spread = jnp.broadcast_to(mine[r * per : (r + 1) * per, None, :], (per, P1, DH)).reshape(FB, DH)
                g_ref[r * FB : (r + 1) * FB, :] = part + spread


def forward(seq_count, pos, q, k, v, left, right, near, far, bias, half):
    tokens, feats = q.shape[0], q.shape[1] // HALVES
    heads, blocks = feats // DH, tokens // FB
    tok = pl.BlockSpec((tokens, DH), lambda h, *_: (0, half * heads + h))
    lev = lambda a: pl.BlockSpec((2, a.shape[1], DH), lambda h, *_: (0, 0, h))
    far_spec = pl.BlockSpec((2, far.shape[1], DH), lambda h, *_: (0, 0, half * heads + h))
    bias_spec = pl.BlockSpec(bias.shape, lambda h, *_: (0, 0, 0))
    return pl.pallas_call(
        functools.partial(fwd_kernel, seq_count),
        grid_spec=pltpu.PrefetchScalarGridSpec(
            num_scalar_prefetch=1,
            grid=(heads,),
            in_specs=[tok, tok, tok, lev(left), lev(right), lev(near), far_spec, bias_spec],
            out_specs=[
                pl.BlockSpec((tokens, DH), lambda h, *_: (0, h)),
                pl.BlockSpec((DH, tokens), lambda h, *_: (h, 0)),
                pl.BlockSpec((1, 1, tokens), lambda h, *_: (h, 0, 0)),
            ],
        ),
        out_shape=[
            jax.ShapeDtypeStruct((tokens, feats), BF),
            jax.ShapeDtypeStruct((feats, tokens), BF),
            jax.ShapeDtypeStruct((heads, 1, tokens), F32),
        ],
        compiler_params=params(BIG),
        cost_estimate=SMALL,
        name="attend",
    )(pos, *pinned(q, k, v, left, right, near, far, bias))


def backward(seq_count, pos, q, k, v, left, right, near, far, bias, do, att, lse):
    tokens, feats = q.shape
    heads = feats // DH
    halo, nr, fr = left.shape[1], near.shape[1], far.shape[1]
    coarse = 3 * nr + fr
    tok = pl.BlockSpec((tokens, DH), lambda h, *_: (0, h))
    lev = lambda r: pl.BlockSpec((2, r, DH), lambda h, *_: (0, 0, h))
    return pl.pallas_call(
        functools.partial(bwd_kernel, seq_count),
        grid_spec=pltpu.PrefetchScalarGridSpec(
            num_scalar_prefetch=1,
            grid=(heads,),
            in_specs=[
                *[tok, tok, tok, lev(halo), lev(halo), lev(nr), lev(fr)],
                pl.BlockSpec(bias.shape, lambda h, *_: (0, 0, 0)),
                *[tok, tok, pl.BlockSpec((1, 1, tokens), lambda h, *_: (h, 0, 0))],
            ],
            out_specs=[tok, tok, tok, lev(halo), lev(halo), lev(fr)],
            scratch_shapes=[
                pltpu.VMEM((tokens + 2 * FB, tokens), BF),
                pltpu.VMEM((tokens + 2 * FB, tokens), BF),
                pltpu.VMEM((coarse, tokens), BF),
                pltpu.VMEM((coarse, tokens), BF),
            ],
        ),
        out_shape=[
            pltpu.HBM((tokens, feats), BF),
            pltpu.HBM((tokens, feats), F32),
            pltpu.HBM((tokens, feats), F32),
            jax.ShapeDtypeStruct((2, halo, feats), BF),
            jax.ShapeDtypeStruct((2, halo, feats), BF),
            jax.ShapeDtypeStruct((2, fr, feats), BF),
        ],
        compiler_params=params(BIG),
        cost_estimate=SMALL,
        name="attend_grad",
    )(pos, *pinned(q, k, v, left, right, near, far, bias), do, att, lse)


def combine_kernel(gk_ref, gv_ref, left_ref, right_ref, far_ref, ok_ref, ov_ref):
    rows, width = gk_ref.shape
    for i, (g_ref, o_ref) in enumerate(((gk_ref, ok_ref), (gv_ref, ov_ref))):
        near = (left_ref[i, FB:].astype(F32) + right_ref[i, FB:].astype(F32)) * (1.0 / P1)
        per = FB // P1
        for r in range(rows // FB):
            part = g_ref[r * FB : (r + 1) * FB]
            part += jnp.broadcast_to(near[r * per : (r + 1) * per, None, :], (per, P1, width)).reshape(FB, width)
            g = r * FB // P2
            part += far_ref[i, g : g + 1] * (1.0 / P2)
            if r == 0:
                part += left_ref[i, :FB].astype(F32)
            if r == rows // FB - 1:
                part += right_ref[i, :FB].astype(F32)
            o_ref[r * FB : (r + 1) * FB] = part.astype(BF)


def combine(gk, gv, from_left, from_right, far):
    rows, feats = gk.shape
    cols = 256
    tok = pl.BlockSpec((rows, cols), lambda j: (0, j))
    lev = lambda r: pl.BlockSpec((2, r, cols), lambda j: (0, 0, j))
    halo = from_left.shape[1]
    return pl.pallas_call(
        combine_kernel,
        grid=(feats // cols,),
        in_specs=[tok, tok, lev(halo), lev(halo), lev(far.shape[1])],
        out_specs=[tok, tok],
        out_shape=[jax.ShapeDtypeStruct((rows, feats), BF)] * 2,
        compiler_params=params(BIG),
        cost_estimate=SMALL,
        name="combine",
    )(*pinned(gk, gv, from_left, from_right, far))


UNITS = 4
ROUTE = ((0, 1, 3), (0, 3, 1), (1, 1, 3), (1, 3, 1))
SECOND = ((1, 3), (3, 1))
SHIFT = (3, 1)


def block_order(pos):
    coord = ((pos >> 3) & 3, (pos >> 1) & 3)
    rows = []
    for u, (axis, k1, k2) in enumerate(ROUTE):
        m1, m2 = SECOND[u // 2]
        first = coord[axis] ^ jnp.array([0, k2, k1, k1 ^ k2], jnp.int32)
        second = coord[1 - axis] ^ jnp.array([0, m2, m1, m1 ^ m2], jnp.int32)
        at = first[:, None] * 4 + second[None, :] if axis == 0 else second[None, :] * 4 + first[:, None]
        rows.append(at.reshape(-1))
    return jnp.stack(rows).astype(jnp.int32)


def weight_kernel(n_units, per, n_recv, pair_out, cols_ref, *refs):
    atts, ogs = refs[:n_units], refs[n_units : n_units + n_units * per]
    recvs = refs[n_units + n_units * per : n_units + n_units * per + n_recv]
    outs = refs[n_units + n_units * per + n_recv :]
    for u in range(n_units):
        for b in range(per):
            res = dot(atts[u][...], ogs[u * per + b][...], 1, 0)
            rows, width = res.shape[0], res.shape[1] // 2
            for z in range(2):
                part = res[:, z * width : (z + 1) * width]
                for r in recvs[u::n_units]:
                    part += r[b, z].astype(F32)
                if pair_out:
                    outs[u // 2][b, z, (u % 2) * rows : (u % 2 + 1) * rows] = part.astype(BF)
                else:
                    outs[u][b, z] = part.astype(BF)


def weight_step(cols, attt, og, width, units, start, count, per, recvs, pair_out):
    tokens = attt[0].shape[1]
    rows = attt[0].shape[0] * HALVES // UNITS
    n = len(units)
    per_half = UNITS // HALVES
    in_specs, args = [], []
    for u in units:
        in_specs.append(pl.BlockSpec((rows, tokens), lambda j, *_, u=u: (u % per_half, 0)))
        args += pinned(attt[u // per_half]) if recvs else [attt[u // per_half]]
    for u in units:
        for b in range(per):
            in_specs.append(pl.BlockSpec((tokens, 2 * width), lambda j, c, u=u, b=b: (0, c[u, start + j * per + b])))
            args += pinned(og)
    for i, step in enumerate(recvs):
        for u in units:
            r, paired = step[u]
            if i < len(recvs) - 1:
                (r,) = pinned(r)
            at = u % 2 if paired else 0
            in_specs.append(pl.BlockSpec((per, 2, rows, width), lambda j, *_, at=at: (start // per + j, 0, at, 0)))
            args.append(r)
    n_out = n // 2 if pair_out else n
    out_rows = 2 * rows if pair_out else rows
    return pl.pallas_call(
        functools.partial(weight_kernel, n, per, len(recvs) * n, pair_out),
        grid_spec=pltpu.PrefetchScalarGridSpec(
            num_scalar_prefetch=1,
            grid=(count // per,),
            in_specs=in_specs,
            out_specs=[pl.BlockSpec((per, 2, out_rows, width), lambda j, *_: (j, 0, 0, 0))] * n_out,
        ),
        out_shape=[jax.ShapeDtypeStruct((count, 2, out_rows, width), BF)] * n_out,
        compiler_params=params(BIG),
        cost_estimate=SMALL,
        name="weight_step",
    )(cols, *args)


def weight_last_kernel(n_recv, table_ref, *refs):
    send_ref, keep_ref = refs[-2:]
    atts, ogs = refs[:UNITS], refs[UNITS : 2 * UNITS]
    recvs = refs[2 * UNITS : 2 * UNITS + n_recv]
    own_first = table_ref[UNITS] == 0
    rows = atts[0].shape[0]
    for u in range(UNITS):
        res = dot(atts[u][...], ogs[u][...], 1, 0)
        width = res.shape[1] // 2
        parts = []
        for z in range(2):
            part = res[:, z * width : (z + 1) * width]
            for r in recvs[u::UNITS]:
                part += r[0, z].astype(F32)
            parts.append(part)
        at = slice(u * rows, (u + 1) * rows)
        keep_ref[at] = jnp.where(own_first, parts[0], parts[1])
        send_ref[at] = jnp.where(own_first, parts[1], parts[0]).astype(BF)


def weight_last(cols, attt, og, width, z, recvs):
    tokens = attt[0].shape[1]
    rows = attt[0].shape[0] * HALVES // UNITS
    per_half = UNITS // HALVES
    table = jnp.concatenate([cols[:, 0], z[None]])
    in_specs, args = [], []
    for u in range(UNITS):
        in_specs.append(pl.BlockSpec((rows, tokens), lambda j, *_, u=u: (u % per_half, 0)))
        args += pinned(attt[u // per_half])
    for u in range(UNITS):
        in_specs.append(pl.BlockSpec((tokens, 2 * width), lambda j, c, u=u: (0, c[u])))
        args += pinned(og)
    for i, step in enumerate(recvs):
        for u in range(UNITS):
            r, paired = step[u]
            if i < len(recvs) - 1:
                (r,) = pinned(r)
            at = u % 2 if paired else 0
            in_specs.append(pl.BlockSpec((1, 2, rows, width), lambda j, c, at=at: (0, 0, at, 0)))
            args.append(r)
    full = pl.BlockSpec((UNITS * rows, width), lambda j, *_: (0, 0))
    return pl.pallas_call(
        functools.partial(weight_last_kernel, len(recvs) * UNITS),
        grid_spec=pltpu.PrefetchScalarGridSpec(num_scalar_prefetch=1, grid=(1,), in_specs=in_specs, out_specs=[full, full]),
        out_shape=[jax.ShapeDtypeStruct((UNITS * rows, width), t) for t in (BF, F32)],
        compiler_params=params(BIG),
        cost_estimate=SMALL,
        name="weight_last",
    )(table, *args)


def project_kernel(og_ref, w_ref, o_ref, acc_ref):
    step = pl.program_id(0)
    part = dot(og_ref[...], w_ref[...], 1, 1)

    @pl.when(step == 0)
    def _():
        acc_ref[...] = part

    @pl.when(step > 0)
    def _():
        acc_ref[...] += part

    @pl.when(step == pl.num_programs(0) - 1)
    def _():
        o_ref[...] = acc_ref[...].astype(BF)


def project(og, w):
    tokens, feats = og.shape[0], w.shape[0]
    n = 1024
    return pl.pallas_call(
        project_kernel,
        grid=(w.shape[1] // n,),
        in_specs=[pl.BlockSpec((tokens, n), lambda s: (0, s)), pl.BlockSpec((feats, n), lambda s: (0, s))],
        out_specs=pl.BlockSpec((tokens, feats), lambda s: (0, 0)),
        out_shape=pltpu.HBM((tokens, feats), BF),
        scratch_shapes=[pltpu.VMEM((tokens, feats), F32)],
        compiler_params=params(BIG),
        cost_estimate=SMALL,
        name="project",
    )(*pinned(og, w))


def layer_kernel(cols_ref, att_ref, w_ref, *part_refs):
    res = dot(att_ref[...], w_ref[...], 1, 0).astype(BF)
    top_ref, bottom_ref, *rest = part_refs
    rows = top_ref.shape[0]

    @pl.when(pl.program_id(0) == 0)
    def _():
        top_ref[...] = res[:rows]
        bottom_ref[...] = res[rows:]

    for i, ref in enumerate(rest):

        @pl.when(pl.program_id(0) == i + 1)
        def _(ref=ref):
            ref[...] = res


def layer_parts(cols, att, w, width):
    tokens, feats = att.shape
    parts = cols.shape[0]
    whole = lambda r, c: pl.BlockSpec((r, c), lambda s, *_: (0, 0))
    return pl.pallas_call(
        layer_kernel,
        grid_spec=pltpu.PrefetchScalarGridSpec(
            num_scalar_prefetch=1,
            grid=(parts,),
            in_specs=[whole(tokens, feats), pl.BlockSpec((feats, width), lambda s, c: (0, c[s]))],
            out_specs=[whole(tokens // 2, width)] * 2 + [whole(tokens, width)] * (parts - 1),
        ),
        out_shape=[
            *[jax.ShapeDtypeStruct((tokens // 2, width), BF)] * 2,
            jax.ShapeDtypeStruct((tokens, width), BF),
            *[pltpu.HBM((tokens, width), BF)] * (parts - 2),
        ],
        compiler_params=params(BIG),
        cost_estimate=SMALL,
        name="layer_parts",
    )(cols, att, *pinned(w))


def swap(x, axis, bits):
    n = lax.axis_size(axis)
    return lax.ppermute(x, axis, [(i, i ^ bits) for i in range(n)])


def after(x, *deps):
    return lax.optimization_barrier((x, *deps))[0]


def add(a, b):
    return (a.astype(F32) + b.astype(F32)).astype(BF)


def own_rows(x, pos, seq_count):
    bit = seq_count // 2
    while bit:
        low = (pos & bit) == 0
        half = x.shape[1] // 2
        a, b = x[:, :half], x[:, half:]
        got = swap(jnp.where(low, b, a), "seq", bit)
        x = jnp.where(low, a, b).astype(F32) + got.astype(F32)
        bit //= 2
        if bit:
            x = x.astype(BF)
    return x


def shards(queries, token_keys, token_values, out_weight, out_grad):
    pos = lax.axis_index("seq").astype(jnp.int32)
    tp = lax.axis_index("tp").astype(jnp.int32)
    seq_count, tp_count = lax.axis_size("seq"), lax.axis_size("tp")
    tokens, feats = queries.shape
    width = out_weight.shape[1]
    pos1 = pos[None]
    right_perm = [(i, i + 1) for i in range(seq_count - 1)]
    left_perm = [(i + 1, i) for i in range(seq_count - 1)]

    near, far_own, to_left, to_right = pool(token_keys, token_values, 0)
    from_left = lax.ppermute(to_right, "seq", right_perm)
    from_right = lax.ppermute(to_left, "seq", left_perm)
    attn_grad = project(after(out_grad, far_own), out_weight)
    far_all = jnp.broadcast_to(after(far_own, attn_grad), (seq_count, *far_own.shape))
    far_all = lax.all_to_all(far_all, "seq", 0, 0, tiled=True)
    far = jnp.moveaxis(far_all, 0, 1).reshape(2, -1, feats)
    bias = level_bias(pos, tokens // FB, near.shape[1], far.shape[1], tokens, seq_count)
    att, attt, lse = forward(
        seq_count, pos1, after(queries, attn_grad), token_keys, token_values, from_left, from_right, near, far, bias, 0
    )

    part = width // seq_count
    cols = block_order(pos)
    every = list(range(UNITS))
    recv1, recv2, recv3, recv4 = ([None] * UNITS for _ in range(4))
    attt = [attt]

    def first_axis(step, dep):
        start, per = (8, 2) if step == 0 else (4, 2)
        got = [recv1][:step]
        out = weight_step(after(cols, *dep), attt, out_grad, part, every, start, start, per, got, False)
        for u, x in enumerate(out):
            (recv1, recv2)[step][u] = (swap(x, "seq", ROUTE[u][1 + step] << SHIFT[ROUTE[u][0]]), False)
        return out

    def second_axis(step, dep):
        start = 2 - step
        got = [recv1, recv2, recv3][: 2 + step]
        out = weight_step(after(cols, *dep), attt, out_grad, part, every, start, start, start, got, True)
        for p, x in enumerate(out):
            moved = swap(x, "seq", SECOND[p][step] << SHIFT[1 - ROUTE[2 * p][0]])
            (recv3, recv4)[step][2 * p : 2 * p + 2] = [(moved, True)] * 2
        return out

    out = first_axis(0, [])
    dq, gk, gv, sl, sr, gfar = backward(
        seq_count, pos1, after(queries, *out), token_keys, token_values, from_left, from_right, near, far, bias, attn_grad, att, lse
    )
    back_left = lax.ppermute(sr, "seq", right_perm)
    back_right = lax.ppermute(sl, "seq", left_perm)
    out = first_axis(1, [gfar])

    c, zl = tp & 1, tp >> 1
    lwidth = width // tp_count
    lcols = jnp.stack([zl ^ 1, zl]) * 2
    lorder = jnp.concatenate([lcols + (c ^ 1), lcols + c])
    top_send, bottom_send, own_send, far_keep, own_keep = layer_parts(lorder, after(att, *out), out_weight, lwidth)
    far_got = jnp.concatenate([swap(top_send, "tp", 1), swap(bottom_send, "tp", 1)])
    own_got = swap(own_send, "tp", 1)
    out = second_axis(0, [top_send, back_left, back_right])
    lsend2 = add(after(far_keep, *out), far_got)
    lgot2 = swap(lsend2, "tp", 2)
    far_parts = jnp.moveaxis(after(gfar, *out).reshape(2, seq_count, -1, feats), 1, 0)
    far_sum = lax.all_to_all(far_parts, "seq", 0, 0, tiled=True).astype(F32).sum(axis=0)
    out = second_axis(1, [*out])
    got = [recv1, recv2, recv3, recv4]
    zsend, zkeep = weight_last(cols, attt, out_grad, part, pos & 1, got)
    zgot = swap(zsend, "seq", 1)
    layer_out = (own_keep.astype(F32) + own_got.astype(F32) + lgot2.astype(F32)).astype(BF)
    key_grad, value_grad = combine(gk, gv, back_left, back_right, far_sum)
    weight_grad = (zkeep + zgot.astype(F32)) * (1.0 / math.sqrt(tokens * seq_count))
    return layer_out, dq, key_grad, value_grad, weight_grad


def solution(mesh):
    return jax.shard_map(
        shards,
        mesh=mesh,
        in_specs=(P("seq", "tp"), P("seq", "tp"), P("seq", "tp"), P("tp", None), P("seq", None)),
        out_specs=(P("seq", "tp"), P("seq", "tp"), P("seq", "tp"), P("seq", "tp"), P("tp", "seq")),
        check_vma=False,
    )
```

```python
import functools
import math

import jax
import jax.numpy as jnp
from jax import lax
from jax.experimental import pallas as pl
from jax.experimental.pallas import tpu as pltpu
from jax.sharding import PartitionSpec as P

DH = 128
FB = 128
P1 = 16
P2 = 256
BF = jnp.bfloat16
F32 = jnp.float32
NEG = -1e30
LOG2E = math.log2(math.e)
MB = 1024 * 1024
HALVES = 1
BIG = 20
SMALL = pl.CostEstimate(flops=1000, bytes_accessed=1000, transcendentals=0)


def dot(a, b, ca, cb):
    return lax.dot_general(a, b, (((ca,), (cb,)), ((), ())), preferred_element_type=F32)


def pinned(*args):
    return [pltpu.with_memory_space_constraint(a, pltpu.HBM) for a in args]


def params(limit):
    return pltpu.CompilerParams(vmem_limit_bytes=limit * MB)


def pool_kernel(k_ref, v_ref, near_ref, far_ref, left_ref, right_ref):
    rows = k_ref.shape[0]
    for i, ref in enumerate((k_ref, v_ref)):
        x = ref[...].astype(F32)
        s16 = x.reshape(rows // P1, P1, x.shape[1]).sum(axis=1)
        near = (s16 * (1.0 / P1)).astype(BF)
        far = s16.reshape(rows // P2, P2 // P1, x.shape[1]).sum(axis=1) * (1.0 / P2)
        near_ref[i] = near
        far_ref[i] = far.astype(BF)
        left_ref[i, :FB] = ref[:FB]
        right_ref[i, :FB] = ref[rows - FB :]
        left_ref[i, FB:] = near
        right_ref[i, FB:] = near


def pool(k, v, half):
    rows, feats = k.shape[0], k.shape[1] // HALVES
    nr, fr = rows // P1, rows // P2
    cols = 256
    per = feats // cols
    blk = lambda r: pl.BlockSpec((2, r, cols), lambda j: (0, 0, j))
    out = lambda r: pltpu.HBM((2, r, feats), BF)
    return pl.pallas_call(
        pool_kernel,
        grid=(per,),
        in_specs=[pl.BlockSpec((rows, cols), lambda j: (0, half * per + j))] * 2,
        out_specs=[blk(nr), blk(fr), blk(FB + nr), blk(FB + nr)],
        out_shape=[out(nr), out(fr), out(FB + nr), out(FB + nr)],
        compiler_params=params(BIG),
        cost_estimate=SMALL,
        name="pool",
    )(*pinned(k, v))


def level_bias(position, blocks, pooled_rows, coarse_count, tokens_here, seq_count):
    group_ids = jnp.arange(3 * pooled_rows, dtype=jnp.int32)
    group_dev = group_ids // pooled_rows
    absent = ((group_dev == 0) & (position == 0)) | ((group_dev == 2) & (position == seq_count - 1))
    block_ids = jnp.arange(blocks, dtype=jnp.int32)[:, None]
    distance = group_ids[None, :] * P1 // FB - blocks - block_ids
    near = jnp.where(absent[None, :] | (jnp.abs(distance) <= 1), NEG, math.log(P1) * LOG2E)
    coarse_dev = jnp.arange(coarse_count, dtype=jnp.int32) * P2 // tokens_here
    far = jnp.where(jnp.abs(coarse_dev - position) > 1, math.log(P2) * LOG2E, NEG)
    far = jnp.broadcast_to(far[None, :], (blocks, coarse_count))
    bias = jnp.concatenate([near, far], axis=1).astype(F32)
    return jnp.broadcast_to(bias[:, :, None], (*bias.shape, FB))


def gathered(i, left_ref, own_ref, right_ref, near_ref, far_ref):
    keys = jnp.concatenate([left_ref[i, :FB], own_ref[...], right_ref[i, :FB]], axis=0)
    coarse = jnp.concatenate([left_ref[i, FB:], near_ref[i], right_ref[i, FB:], far_ref[i]], axis=0)
    return keys, coarse


def scores(b, blocks, pos_ref, seq_count, q, keys, coarse_scores, bias_ref):
    scale = LOG2E / math.sqrt(DH)
    qb = q[b * FB : (b + 1) * FB]
    fine = dot(keys[b * FB : (b + 3) * FB], qb, 1, 1) * scale
    if b == 0:
        edge = jnp.where(pos_ref[0] == 0, NEG, 0.0).astype(F32)
        fine = jnp.concatenate([fine[:FB] + edge, fine[FB:]], axis=0)
    if b == blocks - 1:
        edge = jnp.where(pos_ref[0] == seq_count - 1, NEG, 0.0).astype(F32)
        fine = jnp.concatenate([fine[: 2 * FB], fine[2 * FB :] + edge], axis=0)
    coarse = coarse_scores[:, b * FB : (b + 1) * FB] * scale + bias_ref[b]
    return fine, coarse


def fwd_kernel(seq_count, pos_ref, q_ref, k_ref, v_ref, left_ref, right_ref, near_ref, far_ref, bias_ref, att_ref, attt_ref, lse_ref):
    blocks = q_ref.shape[0] // FB
    q = q_ref[...]
    keys, ckeys = gathered(0, left_ref, k_ref, right_ref, near_ref, far_ref)
    vals, cvals = gathered(1, left_ref, v_ref, right_ref, near_ref, far_ref)
    vals_t, cvals_t = vals.T, cvals.T
    csc = dot(ckeys, q, 1, 1)
    raw = [scores(b, blocks, pos_ref, seq_count, q, keys, csc, bias_ref) for b in range(blocks)]
    peaks = [jnp.maximum(fine.max(axis=0, keepdims=True), coarse.max(axis=0, keepdims=True)) for fine, coarse in raw]
    for b, ((fine, coarse), peak) in enumerate(zip(raw, peaks)):
        pf = jnp.exp2(fine - peak)
        pc = jnp.exp2(coarse - peak)
        total = pf.sum(axis=0, keepdims=True) + pc.sum(axis=0, keepdims=True)
        lse_ref[0, :, b * FB : (b + 1) * FB] = peak + jnp.log2(total)
        out_t = dot(vals_t[:, b * FB : (b + 3) * FB], pf.astype(BF), 1, 0) + dot(cvals_t, pc.astype(BF), 1, 0)
        out_t = (out_t * (1.0 / total)).astype(BF)
        attt_ref[:, b * FB : (b + 1) * FB] = out_t
        att_ref[b * FB : (b + 1) * FB, :] = out_t.T


def bwd_kernel(
    seq_count, pos_ref, q_ref, k_ref, v_ref, left_ref, right_ref, near_ref, far_ref, bias_ref, do_ref, att_ref, lse_ref,
    dq_ref, gk_ref, gv_ref, sl_ref, sr_ref, gfar_ref, p_ref, ds_ref, cp_ref, cds_ref,
):
    blocks = q_ref.shape[0] // FB
    own = blocks * FB
    inv = 1.0 / math.sqrt(DH)
    q, do = q_ref[...], do_ref[...]
    keys, ckeys = gathered(0, left_ref, k_ref, right_ref, near_ref, far_ref)
    vals, cvals = gathered(1, left_ref, v_ref, right_ref, near_ref, far_ref)
    keys_t, ckeys_t = keys.T, ckeys.T
    csc = dot(ckeys, q, 1, 1)
    cdp = dot(cvals, do, 1, 1)
    delta_all = (do.astype(F32) * att_ref[...].astype(F32)).T.sum(axis=0, keepdims=True)
    for b in range(blocks):
        cols = slice(b * FB, (b + 1) * FB)
        fine, coarse = scores(b, blocks, pos_ref, seq_count, q, keys, csc, bias_ref)
        lse = lse_ref[0, :, cols]
        delta = delta_all[:, cols]
        pf = jnp.exp2(fine - lse)
        pc = jnp.exp2(coarse - lse)
        dpf = dot(vals[b * FB : (b + 3) * FB], do[cols], 1, 1)
        dsf = (pf * (dpf - delta)).astype(BF)
        dsc = (pc * (cdp[:, cols] - delta)).astype(BF)
        p_ref[b * FB : (b + 3) * FB, cols] = pf.astype(BF)
        ds_ref[b * FB : (b + 3) * FB, cols] = dsf
        cp_ref[:, cols] = pc.astype(BF)
        cds_ref[:, cols] = dsc
        dq_t = dot(keys_t[:, b * FB : (b + 3) * FB], dsf, 1, 0) + dot(ckeys_t, dsc, 1, 0)
        dq_ref[cols, :] = (dq_t * inv).astype(BF).T
    nr = near_ref.shape[1]
    for i, (src, csrc, rhs, mul, g_ref) in enumerate(((ds_ref, cds_ref, q, inv, gk_ref), (p_ref, cp_ref, do, 1.0, gv_ref))):
        cg = dot(csrc[...], rhs, 1, 0) * mul
        sl_ref[i, FB:] = cg[:nr].astype(BF)
        sr_ref[i, FB:] = cg[2 * nr : 3 * nr].astype(BF)
        gfar_ref[i] = cg[3 * nr :].astype(BF)
        mine = cg[nr : 2 * nr] * (1.0 / P1)
        for c in range(blocks + 2):
            lo, hi = max(0, c - 2), min(blocks, c + 1)
            part = dot(src[c * FB : (c + 1) * FB, lo * FB : hi * FB], rhs[lo * FB : hi * FB], 1, 0) * mul
            if c == 0:
                sl_ref[i, :FB] = part.astype(BF)
            elif c == blocks + 1:
                sr_ref[i, :FB] = part.astype(BF)
            else:
                r = c - 1
                per = FB // P1
                spread = jnp.broadcast_to(mine[r * per : (r + 1) * per, None, :], (per, P1, DH)).reshape(FB, DH)
                g_ref[r * FB : (r + 1) * FB, :] = part + spread


def forward(seq_count, pos, q, k, v, left, right, near, far, bias, half):
    tokens, feats = q.shape[0], q.shape[1] // HALVES
    heads, blocks = feats // DH, tokens // FB
    tok = pl.BlockSpec((tokens, DH), lambda h, *_: (0, half * heads + h))
    lev = lambda a: pl.BlockSpec((2, a.shape[1], DH), lambda h, *_: (0, 0, h))
    far_spec = pl.BlockSpec((2, far.shape[1], DH), lambda h, *_: (0, 0, half * heads + h))
    bias_spec = pl.BlockSpec(bias.shape, lambda h, *_: (0, 0, 0))
    return pl.pallas_call(
        functools.partial(fwd_kernel, seq_count),
        grid_spec=pltpu.PrefetchScalarGridSpec(
            num_scalar_prefetch=1,
            grid=(heads,),
            in_specs=[tok, tok, tok, lev(left), lev(right), lev(near), far_spec, bias_spec],
            out_specs=[
                pl.BlockSpec((tokens, DH), lambda h, *_: (0, h)),
                pl.BlockSpec((DH, tokens), lambda h, *_: (h, 0)),
                pl.BlockSpec((1, 1, tokens), lambda h, *_: (h, 0, 0)),
            ],
        ),
        out_shape=[
            pltpu.HBM((tokens, feats), BF),
            jax.ShapeDtypeStruct((feats, tokens), BF),
            jax.ShapeDtypeStruct((heads, 1, tokens), F32),
        ],
        compiler_params=params(BIG),
        cost_estimate=SMALL,
        name="attend",
    )(pos, *pinned(q, k, v, left, right, near, far, bias))


def backward(seq_count, pos, q, k, v, left, right, near, far, bias, do, att, lse):
    tokens, feats = q.shape
    heads = feats // DH
    halo, nr, fr = left.shape[1], near.shape[1], far.shape[1]
    coarse = 3 * nr + fr
    tok = pl.BlockSpec((tokens, DH), lambda h, *_: (0, h))
    lev = lambda r: pl.BlockSpec((2, r, DH), lambda h, *_: (0, 0, h))
    return pl.pallas_call(
        functools.partial(bwd_kernel, seq_count),
        grid_spec=pltpu.PrefetchScalarGridSpec(
            num_scalar_prefetch=1,
            grid=(heads,),
            in_specs=[
                *[tok, tok, tok, lev(halo), lev(halo), lev(nr), lev(fr)],
                pl.BlockSpec(bias.shape, lambda h, *_: (0, 0, 0)),
                *[tok, tok, pl.BlockSpec((1, 1, tokens), lambda h, *_: (h, 0, 0))],
            ],
            out_specs=[tok, tok, tok, lev(halo), lev(halo), lev(fr)],
            scratch_shapes=[
                pltpu.VMEM((tokens + 2 * FB, tokens), BF),
                pltpu.VMEM((tokens + 2 * FB, tokens), BF),
                pltpu.VMEM((coarse, tokens), BF),
                pltpu.VMEM((coarse, tokens), BF),
            ],
        ),
        out_shape=[
            pltpu.HBM((tokens, feats), BF),
            pltpu.HBM((tokens, feats), F32),
            pltpu.HBM((tokens, feats), F32),
            jax.ShapeDtypeStruct((2, halo, feats), BF),
            jax.ShapeDtypeStruct((2, halo, feats), BF),
            jax.ShapeDtypeStruct((2, fr, feats), BF),
        ],
        compiler_params=params(BIG),
        cost_estimate=SMALL,
        name="attend_grad",
    )(pos, *pinned(q, k, v, left, right, near, far, bias, do, att), lse)


def combine_kernel(gk_ref, gv_ref, left_ref, right_ref, far_ref, ok_ref, ov_ref):
    rows, width = gk_ref.shape
    for i, (g_ref, o_ref) in enumerate(((gk_ref, ok_ref), (gv_ref, ov_ref))):
        near = (left_ref[i, FB:].astype(F32) + right_ref[i, FB:].astype(F32)) * (1.0 / P1)
        per = FB // P1
        for r in range(rows // FB):
            part = g_ref[r * FB : (r + 1) * FB]
            part += jnp.broadcast_to(near[r * per : (r + 1) * per, None, :], (per, P1, width)).reshape(FB, width)
            g = r * FB // P2
            part += far_ref[i, g : g + 1] * (1.0 / P2)
            if r == 0:
                part += left_ref[i, :FB].astype(F32)
            if r == rows // FB - 1:
                part += right_ref[i, :FB].astype(F32)
            o_ref[r * FB : (r + 1) * FB] = part.astype(BF)


def combine(gk, gv, from_left, from_right, far):
    rows, feats = gk.shape
    cols = 256
    tok = pl.BlockSpec((rows, cols), lambda j: (0, j))
    lev = lambda r: pl.BlockSpec((2, r, cols), lambda j: (0, 0, j))
    halo = from_left.shape[1]
    return pl.pallas_call(
        combine_kernel,
        grid=(feats // cols,),
        in_specs=[tok, tok, lev(halo), lev(halo), lev(far.shape[1])],
        out_specs=[tok, tok],
        out_shape=[jax.ShapeDtypeStruct((rows, feats), BF)] * 2,
        compiler_params=params(BIG),
        cost_estimate=SMALL,
        name="combine",
    )(*pinned(gk, gv, from_left, from_right, far))


UNITS = 4
ROUTE = ((0, 1, 3), (0, 3, 1), (1, 1, 3), (1, 3, 1))
SECOND = ((1, 3), (3, 1))
SHIFT = (3, 1)


def block_order(pos):
    coord = ((pos >> 3) & 3, (pos >> 1) & 3)
    rows = []
    for u, (axis, k1, k2) in enumerate(ROUTE):
        m1, m2 = SECOND[u // 2]
        first = coord[axis] ^ jnp.array([0, k2, k1, k1 ^ k2], jnp.int32)
        second = coord[1 - axis] ^ jnp.array([0, m2, m1, m1 ^ m2], jnp.int32)
        at = first[:, None] * 4 + second[None, :] if axis == 0 else second[None, :] * 4 + first[:, None]
        rows.append(at.reshape(-1))
    return jnp.stack(rows).astype(jnp.int32)


def weight_kernel(n_units, per, n_recv, pair_out, cols_ref, *refs):
    atts, ogs = refs[:n_units], refs[n_units : n_units + n_units * per]
    recvs = refs[n_units + n_units * per : n_units + n_units * per + n_recv]
    outs = refs[n_units + n_units * per + n_recv :]
    for u in range(n_units):
        for b in range(per):
            res = dot(atts[u][...], ogs[u * per + b][...], 1, 0)
            rows, width = res.shape[0], res.shape[1] // 2
            for z in range(2):
                part = res[:, z * width : (z + 1) * width]
                for r in recvs[u::n_units]:
                    part += r[b, z].astype(F32)
                if pair_out:
                    outs[u // 2][b, z, (u % 2) * rows : (u % 2 + 1) * rows] = part.astype(BF)
                else:
                    outs[u][b, z] = part.astype(BF)


def weight_step(cols, attt, og, width, units, start, count, per, recvs, pair_out):
    tokens = attt[0].shape[1]
    rows = attt[0].shape[0] * HALVES // UNITS
    n = len(units)
    per_half = UNITS // HALVES
    in_specs, args = [], []
    for u in units:
        in_specs.append(pl.BlockSpec((rows, tokens), lambda j, *_, u=u: (u % per_half, 0)))
        args += pinned(attt[u // per_half]) if recvs else [attt[u // per_half]]
    for u in units:
        for b in range(per):
            in_specs.append(pl.BlockSpec((tokens, 2 * width), lambda j, c, u=u, b=b: (0, c[u, start + j * per + b])))
            args += pinned(og)
    for i, step in enumerate(recvs):
        for u in units:
            r, paired = step[u]
            if i < len(recvs) - 1:
                (r,) = pinned(r)
            at = u % 2 if paired else 0
            in_specs.append(pl.BlockSpec((per, 2, rows, width), lambda j, *_, at=at: (start // per + j, 0, at, 0)))
            args.append(r)
    n_out = n // 2 if pair_out else n
    out_rows = 2 * rows if pair_out else rows
    return pl.pallas_call(
        functools.partial(weight_kernel, n, per, len(recvs) * n, pair_out),
        grid_spec=pltpu.PrefetchScalarGridSpec(
            num_scalar_prefetch=1,
            grid=(count // per,),
            in_specs=in_specs,
            out_specs=[pl.BlockSpec((per, 2, out_rows, width), lambda j, *_: (j, 0, 0, 0))] * n_out,
        ),
        out_shape=[jax.ShapeDtypeStruct((count, 2, out_rows, width), BF)] * n_out,
        compiler_params=params(BIG),
        cost_estimate=SMALL,
        name="weight_step",
    )(cols, *args)


def weight_last_kernel(n_recv, table_ref, *refs):
    send_ref, keep_ref = refs[-2:]
    atts, ogs = refs[:UNITS], refs[UNITS : 2 * UNITS]
    recvs = refs[2 * UNITS : 2 * UNITS + n_recv]
    own_first = table_ref[UNITS] == 0
    rows = atts[0].shape[0]
    for u in range(UNITS):
        res = dot(atts[u][...], ogs[u][...], 1, 0)
        width = res.shape[1] // 2
        parts = []
        for z in range(2):
            part = res[:, z * width : (z + 1) * width]
            for r in recvs[u::UNITS]:
                part += r[0, z].astype(F32)
            parts.append(part)
        at = slice(u * rows, (u + 1) * rows)
        keep_ref[at] = jnp.where(own_first, parts[0], parts[1])
        send_ref[at] = jnp.where(own_first, parts[1], parts[0]).astype(BF)


def weight_last(cols, attt, og, width, z, recvs):
    tokens = attt[0].shape[1]
    rows = attt[0].shape[0] * HALVES // UNITS
    per_half = UNITS // HALVES
    table = jnp.concatenate([cols[:, 0], z[None]])
    in_specs, args = [], []
    for u in range(UNITS):
        in_specs.append(pl.BlockSpec((rows, tokens), lambda j, *_, u=u: (u % per_half, 0)))
        args += pinned(attt[u // per_half])
    for u in range(UNITS):
        in_specs.append(pl.BlockSpec((tokens, 2 * width), lambda j, c, u=u: (0, c[u])))
        args += pinned(og)
    for i, step in enumerate(recvs):
        for u in range(UNITS):
            r, paired = step[u]
            if i < len(recvs) - 1:
                (r,) = pinned(r)
            at = u % 2 if paired else 0
            in_specs.append(pl.BlockSpec((1, 2, rows, width), lambda j, c, at=at: (0, 0, at, 0)))
            args.append(r)
    full = pl.BlockSpec((UNITS * rows, width), lambda j, *_: (0, 0))
    return pl.pallas_call(
        functools.partial(weight_last_kernel, len(recvs) * UNITS),
        grid_spec=pltpu.PrefetchScalarGridSpec(num_scalar_prefetch=1, grid=(1,), in_specs=in_specs, out_specs=[full, full]),
        out_shape=[jax.ShapeDtypeStruct((UNITS * rows, width), t) for t in (BF, F32)],
        compiler_params=params(BIG),
        cost_estimate=SMALL,
        name="weight_last",
    )(table, *args)


def project_kernel(og_ref, w_ref, o_ref, acc_ref):
    step = pl.program_id(0)
    part = dot(og_ref[...], w_ref[...], 1, 1)

    @pl.when(step == 0)
    def _():
        acc_ref[...] = part

    @pl.when(step > 0)
    def _():
        acc_ref[...] += part

    @pl.when(step == pl.num_programs(0) - 1)
    def _():
        o_ref[...] = acc_ref[...].astype(BF)


def project(og, w):
    tokens, feats = og.shape[0], w.shape[0]
    n = 1024
    return pl.pallas_call(
        project_kernel,
        grid=(w.shape[1] // n,),
        in_specs=[pl.BlockSpec((tokens, n), lambda s: (0, s)), pl.BlockSpec((feats, n), lambda s: (0, s))],
        out_specs=pl.BlockSpec((tokens, feats), lambda s: (0, 0)),
        out_shape=pltpu.HBM((tokens, feats), BF),
        scratch_shapes=[pltpu.VMEM((tokens, feats), F32)],
        compiler_params=params(BIG),
        cost_estimate=SMALL,
        name="project",
    )(*pinned(og, w))


def layer_kernel(cols_ref, att_ref, w_ref, *part_refs):
    res = dot(att_ref[...], w_ref[...], 1, 0).astype(BF)
    top_ref, bottom_ref, *rest = part_refs
    rows = top_ref.shape[0]

    @pl.when(pl.program_id(0) == 0)
    def _():
        top_ref[...] = res[:rows]
        bottom_ref[...] = res[rows:]

    for i, ref in enumerate(rest):

        @pl.when(pl.program_id(0) == i + 1)
        def _(ref=ref):
            ref[...] = res


def layer_parts(cols, att, w, width):
    tokens, feats = att.shape
    parts = cols.shape[0]
    whole = lambda r, c: pl.BlockSpec((r, c), lambda s, *_: (0, 0))
    return pl.pallas_call(
        layer_kernel,
        grid_spec=pltpu.PrefetchScalarGridSpec(
            num_scalar_prefetch=1,
            grid=(parts,),
            in_specs=[whole(tokens, feats), pl.BlockSpec((feats, width), lambda s, c: (0, c[s]))],
            out_specs=[whole(tokens // 2, width)] * 2 + [whole(tokens, width)] * (parts - 1),
        ),
        out_shape=[
            *[jax.ShapeDtypeStruct((tokens // 2, width), BF)] * 2,
            jax.ShapeDtypeStruct((tokens, width), BF),
            *[pltpu.HBM((tokens, width), BF)] * (parts - 2),
        ],
        compiler_params=params(BIG),
        cost_estimate=SMALL,
        name="layer_parts",
    )(cols, *pinned(att, w))


def swap(x, axis, bits):
    n = lax.axis_size(axis)
    return lax.ppermute(x, axis, [(i, i ^ bits) for i in range(n)])


def after(x, *deps):
    return lax.optimization_barrier((x, *deps))[0]


def add(a, b):
    return (a.astype(F32) + b.astype(F32)).astype(BF)


def own_rows(x, pos, seq_count):
    bit = seq_count // 2
    while bit:
        low = (pos & bit) == 0
        half = x.shape[1] // 2
        a, b = x[:, :half], x[:, half:]
        got = swap(jnp.where(low, b, a), "seq", bit)
        x = jnp.where(low, a, b).astype(F32) + got.astype(F32)
        bit //= 2
        if bit:
            x = x.astype(BF)
    return x


def shards(queries, token_keys, token_values, out_weight, out_grad):
    pos = lax.axis_index("seq").astype(jnp.int32)
    tp = lax.axis_index("tp").astype(jnp.int32)
    seq_count, tp_count = lax.axis_size("seq"), lax.axis_size("tp")
    tokens, feats = queries.shape
    width = out_weight.shape[1]
    pos1 = pos[None]
    right_perm = [(i, i + 1) for i in range(seq_count - 1)]
    left_perm = [(i + 1, i) for i in range(seq_count - 1)]

    near, far_own, to_left, to_right = pool(token_keys, token_values, 0)
    from_left = lax.ppermute(to_right, "seq", right_perm)
    from_right = lax.ppermute(to_left, "seq", left_perm)
    attn_grad = project(after(out_grad, far_own), out_weight)
    far_all = jnp.broadcast_to(after(far_own, attn_grad), (seq_count, *far_own.shape))
    far_all = lax.all_to_all(far_all, "seq", 0, 0, tiled=True)
    far = jnp.moveaxis(far_all, 0, 1).reshape(2, -1, feats)
    bias = level_bias(pos, tokens // FB, near.shape[1], far.shape[1], tokens, seq_count)
    att, attt, lse = forward(
        seq_count, pos1, after(queries, attn_grad), token_keys, token_values, from_left, from_right, near, far, bias, 0
    )

    part = width // seq_count
    cols = block_order(pos)
    every = list(range(UNITS))
    recv1, recv2, recv3, recv4 = ([None] * UNITS for _ in range(4))
    attt = [attt]

    def first_axis(step, dep):
        start, per = (8, 2) if step == 0 else (4, 2)
        got = [recv1][:step]
        out = weight_step(after(cols, *dep), attt, out_grad, part, every, start, start, per, got, False)
        for u, x in enumerate(out):
            (recv1, recv2)[step][u] = (swap(x, "seq", ROUTE[u][1 + step] << SHIFT[ROUTE[u][0]]), False)
        return out

    def second_axis(step, dep):
        start = 2 - step
        got = [recv1, recv2, recv3][: 2 + step]
        out = weight_step(after(cols, *dep), attt, out_grad, part, every, start, start, start, got, True)
        for p, x in enumerate(out):
            moved = swap(x, "seq", SECOND[p][step] << SHIFT[1 - ROUTE[2 * p][0]])
            (recv3, recv4)[step][2 * p : 2 * p + 2] = [(moved, True)] * 2
        return out

    out = first_axis(0, [])
    dq, gk, gv, sl, sr, gfar = backward(
        seq_count, pos1, after(queries, *out), token_keys, token_values, from_left, from_right, near, far, bias, attn_grad, att, lse
    )
    back_left = lax.ppermute(sr, "seq", right_perm)
    back_right = lax.ppermute(sl, "seq", left_perm)
    c, zl = tp & 1, tp >> 1
    lwidth = width // tp_count
    lcols = jnp.stack([zl ^ 1, zl]) * 2
    lorder = jnp.concatenate([lcols + (c ^ 1), lcols + c])
    top_send, bottom_send, own_send, far_keep, own_keep = layer_parts(lorder, after(att, gfar), out_weight, lwidth)
    far_got = jnp.concatenate([swap(top_send, "tp", 1), swap(bottom_send, "tp", 1)])
    own_got = swap(own_send, "tp", 1)
    out = first_axis(1, [top_send])

    out = second_axis(0, [*out, back_left, back_right])
    lsend2 = add(after(far_keep, *out), far_got)
    lgot2 = swap(lsend2, "tp", 2)
    far_parts = jnp.moveaxis(after(gfar, *out).reshape(2, seq_count, -1, feats), 1, 0)
    far_sum = lax.all_to_all(far_parts, "seq", 0, 0, tiled=True).astype(F32).sum(axis=0)
    out = second_axis(1, [*out])
    got = [recv1, recv2, recv3, recv4]
    zsend, zkeep = weight_last(cols, attt, out_grad, part, pos & 1, got)
    zgot = swap(zsend, "seq", 1)
    layer_out = (own_keep.astype(F32) + own_got.astype(F32) + lgot2.astype(F32)).astype(BF)
    key_grad, value_grad = combine(gk, gv, back_left, back_right, far_sum)
    weight_grad = (zkeep + zgot.astype(F32)) * (1.0 / math.sqrt(tokens * seq_count))
    return layer_out, dq, key_grad, value_grad, weight_grad


def solution(mesh):
    return jax.shard_map(
        shards,
        mesh=mesh,
        in_specs=(P("seq", "tp"), P("seq", "tp"), P("seq", "tp"), P("tp", None), P("seq", None)),
        out_specs=(P("seq", "tp"), P("seq", "tp"), P("seq", "tp"), P("seq", "tp"), P("tp", "seq")),
        check_vma=False,
    )
```

```python
import functools
import math

import jax
import jax.numpy as jnp
from jax import lax
from jax.experimental import pallas as pl
from jax.experimental.pallas import tpu as pltpu
from jax.sharding import PartitionSpec as P

DH = 128
FB = 128
P1 = 16
P2 = 256
BF = jnp.bfloat16
F32 = jnp.float32
NEG = -1e30
LOG2E = math.log2(math.e)
MB = 1024 * 1024
HALVES = 1
BIG = 20
SMALL = pl.CostEstimate(flops=1000, bytes_accessed=1000, transcendentals=0)


def dot(a, b, ca, cb):
    return lax.dot_general(a, b, (((ca,), (cb,)), ((), ())), preferred_element_type=F32)


def pinned(*args):
    return [pltpu.with_memory_space_constraint(a, pltpu.HBM) for a in args]


def params(limit):
    return pltpu.CompilerParams(vmem_limit_bytes=limit * MB)


def pool_kernel(k_ref, v_ref, near_ref, far_ref, left_ref, right_ref):
    rows = k_ref.shape[0]
    for i, ref in enumerate((k_ref, v_ref)):
        x = ref[...].astype(F32)
        s16 = x.reshape(rows // P1, P1, x.shape[1]).sum(axis=1)
        near = (s16 * (1.0 / P1)).astype(BF)
        far = s16.reshape(rows // P2, P2 // P1, x.shape[1]).sum(axis=1) * (1.0 / P2)
        near_ref[i] = near
        far_ref[i] = far.astype(BF)
        left_ref[i, :FB] = ref[:FB]
        right_ref[i, :FB] = ref[rows - FB :]
        left_ref[i, FB:] = near
        right_ref[i, FB:] = near


def pool(k, v, half):
    rows, feats = k.shape[0], k.shape[1] // HALVES
    nr, fr = rows // P1, rows // P2
    cols = 256
    per = feats // cols
    blk = lambda r: pl.BlockSpec((2, r, cols), lambda j: (0, 0, j))
    out = lambda r: pltpu.HBM((2, r, feats), BF)
    return pl.pallas_call(
        pool_kernel,
        grid=(per,),
        in_specs=[pl.BlockSpec((rows, cols), lambda j: (0, half * per + j))] * 2,
        out_specs=[blk(nr), blk(fr), blk(FB + nr), blk(FB + nr)],
        out_shape=[out(nr), out(fr), out(FB + nr), out(FB + nr)],
        compiler_params=params(BIG),
        cost_estimate=SMALL,
        name="pool",
    )(*pinned(k, v))


def level_bias(position, blocks, pooled_rows, coarse_count, tokens_here, seq_count):
    group_ids = jnp.arange(3 * pooled_rows, dtype=jnp.int32)
    group_dev = group_ids // pooled_rows
    absent = ((group_dev == 0) & (position == 0)) | ((group_dev == 2) & (position == seq_count - 1))
    block_ids = jnp.arange(blocks, dtype=jnp.int32)[:, None]
    distance = group_ids[None, :] * P1 // FB - blocks - block_ids
    near = jnp.where(absent[None, :] | (jnp.abs(distance) <= 1), NEG, math.log(P1) * LOG2E)
    coarse_dev = jnp.arange(coarse_count, dtype=jnp.int32) * P2 // tokens_here
    far = jnp.where(jnp.abs(coarse_dev - position) > 1, math.log(P2) * LOG2E, NEG)
    far = jnp.broadcast_to(far[None, :], (blocks, coarse_count))
    bias = jnp.concatenate([near, far], axis=1).astype(F32)
    return jnp.broadcast_to(bias[:, :, None], (*bias.shape, FB))


def gathered(i, left_ref, own_ref, right_ref, near_ref, far_ref):
    keys = jnp.concatenate([left_ref[i, :FB], own_ref[...], right_ref[i, :FB]], axis=0)
    coarse = jnp.concatenate([left_ref[i, FB:], near_ref[i], right_ref[i, FB:], far_ref[i]], axis=0)
    return keys, coarse


def scores(b, blocks, pos_ref, seq_count, q, keys, coarse_scores, bias_ref):
    scale = LOG2E / math.sqrt(DH)
    qb = q[b * FB : (b + 1) * FB]
    fine = dot(keys[b * FB : (b + 3) * FB], qb, 1, 1) * scale
    if b == 0:
        edge = jnp.where(pos_ref[0] == 0, NEG, 0.0).astype(F32)
        fine = jnp.concatenate([fine[:FB] + edge, fine[FB:]], axis=0)
    if b == blocks - 1:
        edge = jnp.where(pos_ref[0] == seq_count - 1, NEG, 0.0).astype(F32)
        fine = jnp.concatenate([fine[: 2 * FB], fine[2 * FB :] + edge], axis=0)
    coarse = coarse_scores[:, b * FB : (b + 1) * FB] * scale + bias_ref[b]
    return fine, coarse


def fwd_kernel(seq_count, pos_ref, q_ref, k_ref, v_ref, left_ref, right_ref, near_ref, far_ref, bias_ref, att_ref, attt_ref, lse_ref):
    blocks = q_ref.shape[0] // FB
    q = q_ref[...]
    keys, ckeys = gathered(0, left_ref, k_ref, right_ref, near_ref, far_ref)
    vals, cvals = gathered(1, left_ref, v_ref, right_ref, near_ref, far_ref)
    vals_t, cvals_t = vals.T, cvals.T
    csc = dot(ckeys, q, 1, 1)
    raw = [scores(b, blocks, pos_ref, seq_count, q, keys, csc, bias_ref) for b in range(blocks)]
    peaks = [jnp.maximum(fine.max(axis=0, keepdims=True), coarse.max(axis=0, keepdims=True)) for fine, coarse in raw]
    for b, ((fine, coarse), peak) in enumerate(zip(raw, peaks)):
        pf = jnp.exp2(fine - peak)
        pc = jnp.exp2(coarse - peak)
        total = pf.sum(axis=0, keepdims=True) + pc.sum(axis=0, keepdims=True)
        lse_ref[0, :, b * FB : (b + 1) * FB] = peak + jnp.log2(total)
        out_t = dot(vals_t[:, b * FB : (b + 3) * FB], pf.astype(BF), 1, 0) + dot(cvals_t, pc.astype(BF), 1, 0)
        out_t = (out_t * (1.0 / total)).astype(BF)
        attt_ref[:, b * FB : (b + 1) * FB] = out_t
        att_ref[b * FB : (b + 1) * FB, :] = out_t.T


def bwd_kernel(
    seq_count, pos_ref, q_ref, k_ref, v_ref, left_ref, right_ref, near_ref, far_ref, bias_ref, do_ref, att_ref, lse_ref,
    dq_ref, gk_ref, gv_ref, sl_ref, sr_ref, gfar_ref, p_ref, ds_ref, cp_ref, cds_ref,
):
    blocks = q_ref.shape[0] // FB
    own = blocks * FB
    inv = 1.0 / math.sqrt(DH)
    q, do = q_ref[...], do_ref[...]
    keys, ckeys = gathered(0, left_ref, k_ref, right_ref, near_ref, far_ref)
    vals, cvals = gathered(1, left_ref, v_ref, right_ref, near_ref, far_ref)
    keys_t, ckeys_t = keys.T, ckeys.T
    csc = dot(ckeys, q, 1, 1)
    cdp = dot(cvals, do, 1, 1)
    delta_all = (do.astype(F32) * att_ref[...].astype(F32)).T.sum(axis=0, keepdims=True)
    for b in range(blocks):
        cols = slice(b * FB, (b + 1) * FB)
        fine, coarse = scores(b, blocks, pos_ref, seq_count, q, keys, csc, bias_ref)
        lse = lse_ref[0, :, cols]
        delta = delta_all[:, cols]
        pf = jnp.exp2(fine - lse)
        pc = jnp.exp2(coarse - lse)
        dpf = dot(vals[b * FB : (b + 3) * FB], do[cols], 1, 1)
        dsf = (pf * (dpf - delta)).astype(BF)
        dsc = (pc * (cdp[:, cols] - delta)).astype(BF)
        p_ref[b * FB : (b + 3) * FB, cols] = pf.astype(BF)
        ds_ref[b * FB : (b + 3) * FB, cols] = dsf
        cp_ref[:, cols] = pc.astype(BF)
        cds_ref[:, cols] = dsc
        dq_t = dot(keys_t[:, b * FB : (b + 3) * FB], dsf, 1, 0) + dot(ckeys_t, dsc, 1, 0)
        dq_ref[cols, :] = (dq_t * inv).astype(BF).T
    nr = near_ref.shape[1]
    for i, (src, csrc, rhs, mul, g_ref) in enumerate(((ds_ref, cds_ref, q, inv, gk_ref), (p_ref, cp_ref, do, 1.0, gv_ref))):
        cg = dot(csrc[...], rhs, 1, 0) * mul
        sl_ref[i, FB:] = cg[:nr].astype(BF)
        sr_ref[i, FB:] = cg[2 * nr : 3 * nr].astype(BF)
        gfar_ref[i] = cg[3 * nr :].astype(BF)
        mine = cg[nr : 2 * nr] * (1.0 / P1)
        for c in range(blocks + 2):
            lo, hi = max(0, c - 2), min(blocks, c + 1)
            part = dot(src[c * FB : (c + 1) * FB, lo * FB : hi * FB], rhs[lo * FB : hi * FB], 1, 0) * mul
            if c == 0:
                sl_ref[i, :FB] = part.astype(BF)
            elif c == blocks + 1:
                sr_ref[i, :FB] = part.astype(BF)
            else:
                r = c - 1
                per = FB // P1
                spread = jnp.broadcast_to(mine[r * per : (r + 1) * per, None, :], (per, P1, DH)).reshape(FB, DH)
                g_ref[r * FB : (r + 1) * FB, :] = part + spread


def forward(seq_count, pos, q, k, v, left, right, near, far, bias, half):
    tokens, feats = q.shape[0], q.shape[1] // HALVES
    heads, blocks = feats // DH, tokens // FB
    tok = pl.BlockSpec((tokens, DH), lambda h, *_: (0, half * heads + h))
    lev = lambda a: pl.BlockSpec((2, a.shape[1], DH), lambda h, *_: (0, 0, h))
    far_spec = pl.BlockSpec((2, far.shape[1], DH), lambda h, *_: (0, 0, half * heads + h))
    bias_spec = pl.BlockSpec(bias.shape, lambda h, *_: (0, 0, 0))
    return pl.pallas_call(
        functools.partial(fwd_kernel, seq_count),
        grid_spec=pltpu.PrefetchScalarGridSpec(
            num_scalar_prefetch=1,
            grid=(heads,),
            in_specs=[tok, tok, tok, lev(left), lev(right), lev(near), far_spec, bias_spec],
            out_specs=[
                pl.BlockSpec((tokens, DH), lambda h, *_: (0, h)),
                pl.BlockSpec((DH, tokens), lambda h, *_: (h, 0)),
                pl.BlockSpec((1, 1, tokens), lambda h, *_: (h, 0, 0)),
            ],
        ),
        out_shape=[
            pltpu.HBM((tokens, feats), BF),
            jax.ShapeDtypeStruct((feats, tokens), BF),
            jax.ShapeDtypeStruct((heads, 1, tokens), F32),
        ],
        compiler_params=params(BIG),
        cost_estimate=SMALL,
        name="attend",
    )(pos, *pinned(q, k, v, left, right, near, far, bias))


def backward(seq_count, pos, q, k, v, left, right, near, far, bias, do, att, lse):
    tokens, feats = q.shape
    heads = feats // DH
    halo, nr, fr = left.shape[1], near.shape[1], far.shape[1]
    coarse = 3 * nr + fr
    tok = pl.BlockSpec((tokens, DH), lambda h, *_: (0, h))
    lev = lambda r: pl.BlockSpec((2, r, DH), lambda h, *_: (0, 0, h))
    return pl.pallas_call(
        functools.partial(bwd_kernel, seq_count),
        grid_spec=pltpu.PrefetchScalarGridSpec(
            num_scalar_prefetch=1,
            grid=(heads,),
            in_specs=[
                *[tok, tok, tok, lev(halo), lev(halo), lev(nr), lev(fr)],
                pl.BlockSpec(bias.shape, lambda h, *_: (0, 0, 0)),
                *[tok, tok, pl.BlockSpec((1, 1, tokens), lambda h, *_: (h, 0, 0))],
            ],
            out_specs=[tok, tok, tok, lev(halo), lev(halo), lev(fr)],
            scratch_shapes=[
                pltpu.VMEM((tokens + 2 * FB, tokens), BF),
                pltpu.VMEM((tokens + 2 * FB, tokens), BF),
                pltpu.VMEM((coarse, tokens), BF),
                pltpu.VMEM((coarse, tokens), BF),
            ],
        ),
        out_shape=[
            pltpu.HBM((tokens, feats), BF),
            pltpu.HBM((tokens, feats), F32),
            pltpu.HBM((tokens, feats), F32),
            jax.ShapeDtypeStruct((2, halo, feats), BF),
            jax.ShapeDtypeStruct((2, halo, feats), BF),
            jax.ShapeDtypeStruct((2, fr, feats), BF),
        ],
        compiler_params=params(BIG),
        cost_estimate=SMALL,
        name="attend_grad",
    )(pos, *pinned(q, k, v, left, right, near, far, bias, do, att), lse)


def combine_kernel(gk_ref, gv_ref, left_ref, right_ref, far_ref, ok_ref, ov_ref):
    rows, width = gk_ref.shape
    for i, (g_ref, o_ref) in enumerate(((gk_ref, ok_ref), (gv_ref, ov_ref))):
        near = (left_ref[i, FB:].astype(F32) + right_ref[i, FB:].astype(F32)) * (1.0 / P1)
        per = FB // P1
        for r in range(rows // FB):
            part = g_ref[r * FB : (r + 1) * FB]
            part += jnp.broadcast_to(near[r * per : (r + 1) * per, None, :], (per, P1, width)).reshape(FB, width)
            g = r * FB // P2
            part += far_ref[i, g : g + 1] * (1.0 / P2)
            if r == 0:
                part += left_ref[i, :FB].astype(F32)
            if r == rows // FB - 1:
                part += right_ref[i, :FB].astype(F32)
            o_ref[r * FB : (r + 1) * FB] = part.astype(BF)


def combine(gk, gv, from_left, from_right, far):
    rows, feats = gk.shape
    cols = 256
    tok = pl.BlockSpec((rows, cols), lambda j: (0, j))
    lev = lambda r: pl.BlockSpec((2, r, cols), lambda j: (0, 0, j))
    halo = from_left.shape[1]
    return pl.pallas_call(
        combine_kernel,
        grid=(feats // cols,),
        in_specs=[tok, tok, lev(halo), lev(halo), lev(far.shape[1])],
        out_specs=[tok, tok],
        out_shape=[jax.ShapeDtypeStruct((rows, feats), BF)] * 2,
        compiler_params=params(BIG),
        cost_estimate=SMALL,
        name="combine",
    )(*pinned(gk, gv, from_left, from_right, far))


UNITS = 4
ROUTE = ((0, 1, 3), (0, 3, 1), (1, 1, 3), (1, 3, 1))
SECOND = ((1, 3), (3, 1))
SHIFT = (3, 1)


def block_order(pos):
    coord = ((pos >> 3) & 3, (pos >> 1) & 3)
    rows = []
    for u, (axis, k1, k2) in enumerate(ROUTE):
        m1, m2 = SECOND[u // 2]
        first = coord[axis] ^ jnp.array([0, k2, k1, k1 ^ k2], jnp.int32)
        second = coord[1 - axis] ^ jnp.array([0, m2, m1, m1 ^ m2], jnp.int32)
        at = first[:, None] * 4 + second[None, :] if axis == 0 else second[None, :] * 4 + first[:, None]
        rows.append(at.reshape(-1))
    return jnp.stack(rows).astype(jnp.int32)


def weight_kernel(n_units, per, n_recv, pair_out, cols_ref, *refs):
    atts, ogs = refs[:n_units], refs[n_units : n_units + n_units * per]
    recvs = refs[n_units + n_units * per : n_units + n_units * per + n_recv]
    outs = refs[n_units + n_units * per + n_recv :]
    for u in range(n_units):
        for b in range(per):
            res = dot(atts[u][...], ogs[u * per + b][...], 1, 0)
            rows, width = res.shape[0], res.shape[1] // 2
            for z in range(2):
                part = res[:, z * width : (z + 1) * width]
                for r in recvs[u::n_units]:
                    part += r[b, z].astype(F32)
                if pair_out:
                    outs[u // 2][b, z, (u % 2) * rows : (u % 2 + 1) * rows] = part.astype(BF)
                else:
                    outs[u][b, z] = part.astype(BF)


def weight_step(cols, attt, og, width, units, start, count, per, recvs, pair_out):
    tokens = attt[0].shape[1]
    rows = attt[0].shape[0] * HALVES // UNITS
    n = len(units)
    per_half = UNITS // HALVES
    in_specs, args = [], []
    for u in units:
        in_specs.append(pl.BlockSpec((rows, tokens), lambda j, *_, u=u: (u % per_half, 0)))
        args += pinned(attt[u // per_half]) if recvs else [attt[u // per_half]]
    for u in units:
        for b in range(per):
            in_specs.append(pl.BlockSpec((tokens, 2 * width), lambda j, c, u=u, b=b: (0, c[u, start + j * per + b])))
            args += pinned(og)
    for i, step in enumerate(recvs):
        for u in units:
            r, paired = step[u]
            if i < len(recvs) - 1:
                (r,) = pinned(r)
            at = u % 2 if paired else 0
            in_specs.append(pl.BlockSpec((per, 2, rows, width), lambda j, *_, at=at: (start // per + j, 0, at, 0)))
            args.append(r)
    n_out = n // 2 if pair_out else n
    out_rows = 2 * rows if pair_out else rows
    return pl.pallas_call(
        functools.partial(weight_kernel, n, per, len(recvs) * n, pair_out),
        grid_spec=pltpu.PrefetchScalarGridSpec(
            num_scalar_prefetch=1,
            grid=(count // per,),
            in_specs=in_specs,
            out_specs=[pl.BlockSpec((per, 2, out_rows, width), lambda j, *_: (j, 0, 0, 0))] * n_out,
        ),
        out_shape=[jax.ShapeDtypeStruct((count, 2, out_rows, width), BF)] * n_out,
        compiler_params=params(BIG),
        cost_estimate=SMALL,
        name="weight_step",
    )(cols, *args)


def weight_last_kernel(n_recv, table_ref, *refs):
    send_ref, keep_ref = refs[-2:]
    atts, ogs = refs[:UNITS], refs[UNITS : 2 * UNITS]
    recvs = refs[2 * UNITS : 2 * UNITS + n_recv]
    own_first = table_ref[UNITS] == 0
    rows = atts[0].shape[0]
    for u in range(UNITS):
        res = dot(atts[u][...], ogs[u][...], 1, 0)
        width = res.shape[1] // 2
        parts = []
        for z in range(2):
            part = res[:, z * width : (z + 1) * width]
            for r in recvs[u::UNITS]:
                part += r[0, z].astype(F32)
            parts.append(part)
        at = slice(u * rows, (u + 1) * rows)
        keep_ref[at] = jnp.where(own_first, parts[0], parts[1])
        send_ref[at] = jnp.where(own_first, parts[1], parts[0]).astype(BF)


def weight_last(cols, attt, og, width, z, recvs):
    tokens = attt[0].shape[1]
    rows = attt[0].shape[0] * HALVES // UNITS
    per_half = UNITS // HALVES
    table = jnp.concatenate([cols[:, 0], z[None]])
    in_specs, args = [], []
    for u in range(UNITS):
        in_specs.append(pl.BlockSpec((rows, tokens), lambda j, *_, u=u: (u % per_half, 0)))
        args += pinned(attt[u // per_half])
    for u in range(UNITS):
        in_specs.append(pl.BlockSpec((tokens, 2 * width), lambda j, c, u=u: (0, c[u])))
        args += pinned(og)
    for i, step in enumerate(recvs):
        for u in range(UNITS):
            r, paired = step[u]
            if i < len(recvs) - 1:
                (r,) = pinned(r)
            at = u % 2 if paired else 0
            in_specs.append(pl.BlockSpec((1, 2, rows, width), lambda j, c, at=at: (0, 0, at, 0)))
            args.append(r)
    full = pl.BlockSpec((UNITS * rows, width), lambda j, *_: (0, 0))
    return pl.pallas_call(
        functools.partial(weight_last_kernel, len(recvs) * UNITS),
        grid_spec=pltpu.PrefetchScalarGridSpec(num_scalar_prefetch=1, grid=(1,), in_specs=in_specs, out_specs=[full, full]),
        out_shape=[jax.ShapeDtypeStruct((UNITS * rows, width), t) for t in (BF, F32)],
        compiler_params=params(BIG),
        cost_estimate=SMALL,
        name="weight_last",
    )(table, *args)


def project_kernel(og_ref, w_ref, o_ref, acc_ref):
    step = pl.program_id(0)
    part = dot(og_ref[...], w_ref[...], 1, 1)

    @pl.when(step == 0)
    def _():
        acc_ref[...] = part

    @pl.when(step > 0)
    def _():
        acc_ref[...] += part

    @pl.when(step == pl.num_programs(0) - 1)
    def _():
        o_ref[...] = acc_ref[...].astype(BF)


def project(og, w):
    tokens, feats = og.shape[0], w.shape[0]
    n = 1024
    return pl.pallas_call(
        project_kernel,
        grid=(w.shape[1] // n,),
        in_specs=[pl.BlockSpec((tokens, n), lambda s: (0, s)), pl.BlockSpec((feats, n), lambda s: (0, s))],
        out_specs=pl.BlockSpec((tokens, feats), lambda s: (0, 0)),
        out_shape=pltpu.HBM((tokens, feats), BF),
        scratch_shapes=[pltpu.VMEM((tokens, feats), F32)],
        compiler_params=params(BIG),
        cost_estimate=SMALL,
        name="project",
    )(*pinned(og, w))


def layer_kernel(cols_ref, att_ref, w_ref, *part_refs):
    res = dot(att_ref[...], w_ref[...], 1, 0).astype(BF)
    top_ref, bottom_ref, *rest = part_refs
    rows = top_ref.shape[0]

    @pl.when(pl.program_id(0) == 0)
    def _():
        top_ref[...] = res[:rows]
        bottom_ref[...] = res[rows:]

    for i, ref in enumerate(rest):

        @pl.when(pl.program_id(0) == i + 1)
        def _(ref=ref):
            ref[...] = res


def layer_parts(cols, att, w, width):
    tokens, feats = att.shape
    parts = cols.shape[0]
    whole = lambda r, c: pl.BlockSpec((r, c), lambda s, *_: (0, 0))
    return pl.pallas_call(
        layer_kernel,
        grid_spec=pltpu.PrefetchScalarGridSpec(
            num_scalar_prefetch=1,
            grid=(parts,),
            in_specs=[whole(tokens, feats), pl.BlockSpec((feats, width), lambda s, c: (0, c[s]))],
            out_specs=[whole(tokens // 2, width)] * 2 + [whole(tokens, width)] * (parts - 1),
        ),
        out_shape=[
            *[jax.ShapeDtypeStruct((tokens // 2, width), BF)] * 2,
            jax.ShapeDtypeStruct((tokens, width), BF),
            *[pltpu.HBM((tokens, width), BF)] * (parts - 2),
        ],
        compiler_params=params(BIG),
        cost_estimate=SMALL,
        name="layer_parts",
    )(cols, *pinned(att, w))


def swap(x, axis, bits):
    n = lax.axis_size(axis)
    return lax.ppermute(x, axis, [(i, i ^ bits) for i in range(n)])


def after(x, *deps):
    return lax.optimization_barrier((x, *deps))[0]


def add(a, b):
    return (a.astype(F32) + b.astype(F32)).astype(BF)


def own_rows(x, pos, seq_count):
    bit = seq_count // 2
    while bit:
        low = (pos & bit) == 0
        half = x.shape[1] // 2
        a, b = x[:, :half], x[:, half:]
        got = swap(jnp.where(low, b, a), "seq", bit)
        x = jnp.where(low, a, b).astype(F32) + got.astype(F32)
        bit //= 2
        if bit:
            x = x.astype(BF)
    return x


def shards(queries, token_keys, token_values, out_weight, out_grad):
    pos = lax.axis_index("seq").astype(jnp.int32)
    tp = lax.axis_index("tp").astype(jnp.int32)
    seq_count, tp_count = lax.axis_size("seq"), lax.axis_size("tp")
    tokens, feats = queries.shape
    width = out_weight.shape[1]
    pos1 = pos[None]
    right_perm = [(i, i + 1) for i in range(seq_count - 1)]
    left_perm = [(i + 1, i) for i in range(seq_count - 1)]

    near, far_own, to_left, to_right = pool(token_keys, token_values, 0)
    from_left = lax.ppermute(to_right, "seq", right_perm)
    from_right = lax.ppermute(to_left, "seq", left_perm)
    attn_grad = project(after(out_grad, far_own), out_weight)
    far_all = jnp.broadcast_to(after(far_own, attn_grad), (seq_count, *far_own.shape))
    far_all = lax.all_to_all(far_all, "seq", 0, 0, tiled=True)
    far = jnp.moveaxis(far_all, 0, 1).reshape(2, -1, feats)
    bias = level_bias(pos, tokens // FB, near.shape[1], far.shape[1], tokens, seq_count)
    att, attt, lse = forward(
        seq_count, pos1, after(queries, attn_grad), token_keys, token_values, from_left, from_right, near, far, bias, 0
    )

    part = width // seq_count
    cols = block_order(pos)
    every = list(range(UNITS))
    recv1, recv2, recv3, recv4 = ([None] * UNITS for _ in range(4))
    attt = [attt]

    def first_axis(step, dep):
        start, per = (8, 4) if step == 0 else (4, 2)
        got = [recv1][:step]
        out = weight_step(after(cols, *dep), attt, out_grad, part, every, start, start, per, got, False)
        for u, x in enumerate(out):
            (recv1, recv2)[step][u] = (swap(x, "seq", ROUTE[u][1 + step] << SHIFT[ROUTE[u][0]]), False)
        return out

    def second_axis(step, dep):
        start = 2 - step
        got = [recv1, recv2, recv3][: 2 + step]
        out = weight_step(after(cols, *dep), attt, out_grad, part, every, start, start, start, got, True)
        for p, x in enumerate(out):
            moved = swap(x, "seq", SECOND[p][step] << SHIFT[1 - ROUTE[2 * p][0]])
            (recv3, recv4)[step][2 * p : 2 * p + 2] = [(moved, True)] * 2
        return out

    out = first_axis(0, [])
    dq, gk, gv, sl, sr, gfar = backward(
        seq_count, pos1, after(queries, *out), token_keys, token_values, from_left, from_right, near, far, bias, attn_grad, att, lse
    )
    back_left = lax.ppermute(sr, "seq", right_perm)
    back_right = lax.ppermute(sl, "seq", left_perm)
    c, zl = tp & 1, tp >> 1
    lwidth = width // tp_count
    lcols = jnp.stack([zl ^ 1, zl]) * 2
    lorder = jnp.concatenate([lcols + (c ^ 1), lcols + c])
    top_send, bottom_send, own_send, far_keep, own_keep = layer_parts(lorder, after(att, gfar), out_weight, lwidth)
    far_got = jnp.concatenate([swap(top_send, "tp", 1), swap(bottom_send, "tp", 1)])
    own_got = swap(own_send, "tp", 1)
    out = first_axis(1, [top_send])

    out = second_axis(0, [*out, back_left, back_right])
    lsend2 = add(after(far_keep, *out), far_got)
    lgot2 = swap(lsend2, "tp", 2)
    far_parts = jnp.moveaxis(after(gfar, *out).reshape(2, seq_count, -1, feats), 1, 0)
    far_sum = lax.all_to_all(far_parts, "seq", 0, 0, tiled=True).astype(F32).sum(axis=0)
    out = second_axis(1, [*out])
    got = [recv1, recv2, recv3, recv4]
    zsend, zkeep = weight_last(cols, attt, out_grad, part, pos & 1, got)
    zgot = swap(zsend, "seq", 1)
    layer_out = (own_keep.astype(F32) + own_got.astype(F32) + lgot2.astype(F32)).astype(BF)
    key_grad, value_grad = combine(gk, gv, back_left, back_right, far_sum)
    weight_grad = (zkeep + zgot.astype(F32)) * (1.0 / math.sqrt(tokens * seq_count))
    return layer_out, dq, key_grad, value_grad, weight_grad


def solution(mesh):
    return jax.shard_map(
        shards,
        mesh=mesh,
        in_specs=(P("seq", "tp"), P("seq", "tp"), P("seq", "tp"), P("tp", None), P("seq", None)),
        out_specs=(P("seq", "tp"), P("seq", "tp"), P("seq", "tp"), P("seq", "tp"), P("tp", "seq")),
        check_vma=False,
    )
```
